32 devices in a mesh: groups: 2 (over x), ha: 16 (over z, y, core).
Axes of the slice: x: 2, y: 2, z: 4, core: 2. Of those that a mesh axis runs over, the one named last changes fastest.
Arguments:
- video: bfloat16 [8, 64, 192, 192], P('groups', 'ha'), parts along dimension 0, may hold values from -6 to 6
- s1_weight: bfloat16 [3, 3, 192, 128], replicated, may hold values from -0.15625 to 0.15625
- t1_weight: bfloat16 [3, 128, 128], replicated, may hold values from -0.3125 to 0.3125
- r1_weight: bfloat16 [2, 2, 128, 256], replicated, may hold values from -0.25 to 0.25
- s2_weight: bfloat16 [3, 3, 256, 256], replicated, may hold values from -0.125 to 0.125
- t2_weight: bfloat16 [3, 256, 256], replicated, may hold values from -0.21875 to 0.21875
- r2_weight: bfloat16 [2, 2, 256, 512], replicated, may hold values from -0.1875 to 0.1875
- attn_gain: bfloat16 [512], replicated, may hold values from 0.5 to 1.5
- w_query: bfloat16 [512, 512], replicated, may hold values from -2.5 to 2.5
- w_key: bfloat16 [512, 512], replicated, may hold values from -0.27 to 0.27
- w_value: bfloat16 [512, 512], replicated, may hold values from -0.25 to 0.25
- w_out: bfloat16 [512, 512], replicated, may hold values from -1 to 1
Outputs:
- encoded: bfloat16 [8, 16, 48, 512], P('groups', 'ha'), parts along dimension 0
The draws below stay inside these ranges and needn't reach their ends.
There are 2 independent parts, one for each index of `groups`. The reference program is written for one: setup_inputs(seed, part) draws one part's arguments, and reference() takes and returns one part's arrays. A program takes and returns all parts, laid end to end along the dimension named above; an argument that names none is the same for every part. Nothing has to cross between parts.
All inputs are finite; a program needn't handle non-finite values.
Results may differ from the reference program's by a relative error of at most 0.018.
Values may be sent and summed in bfloat16 or wider, within the bound.
No kernel may reach another device: no remote copies, remote signals or barrier semaphores. Data moves between devices by JAX's collectives and lax.ppermute only.
A program may use at most 128 MiB of HBM per device.

```python
import math
import jax
import jax.numpy as jnp
from jax import lax

C0 = 192
C1 = 128
C2 = 256
C3 = 512
FRAMES = 4
W = 192
H = 64


def key_base(key):
    raw = jax.random.truncated_normal(jax.random.fold_in(key, 71), -6.0, 6.0, (C3, C3), jnp.float32) / jnp.sqrt(jnp.float32(C3))
    return jnp.clip(raw, -0.27, 0.27)


def draw_w_key(key, part):
    return key_base(key).astype(jnp.bfloat16)


def draw_w_query(key, part):
    noise = jax.random.truncated_normal(jax.random.fold_in(key, 83), -6.0, 6.0, (C3, C3), jnp.float32) * 2.0 / jnp.sqrt(jnp.float32(C3))
    return jnp.clip(noise, -2.5, 2.5).astype(jnp.bfloat16)


def steps_of(own_key, extent, pieces, least, top_value):
    def one(axis_at, parts):
        draws = jax.random.uniform(jax.random.fold_in(jax.random.fold_in(own_key, 6), axis_at), (parts,), jnp.float32, least / len(pieces), top_value / len(pieces))
        return jnp.repeat(jnp.exp(draws), extent[axis_at] // parts).reshape((-1,) + (1,) * (len(extent) - axis_at - 1))

    factor_of = one(*pieces[0])
    for cut in pieces[1:]:
        factor_of = factor_of * one(*cut)
    return factor_of


def gaussian(own_key, extent, scale, most, shards=(), held_as=jnp.bfloat16):
    result = scale * jax.random.normal(own_key, extent, jnp.float32)
    if shards:
        result = result * steps_of(own_key, extent, shards, -0.22, 0.18)
    return jnp.clip(result, -most, most).astype(held_as)


def setup_inputs(seed: int = 0, part: int = 0) -> dict:
    streams_of = jax.random.split(jax.random.key(seed), 13)
    own_keys = jax.random.split(jax.random.fold_in(streams_of[12], part), 13)
    return {
        "video": gaussian(own_keys[0], (FRAMES, H, W, C0), 1.0, 6.0, ((1, 16),)),
        "s1_weight": gaussian(streams_of[1], (3, 3, C0, C1), (9 * C0) ** -0.5, 0.15625),
        "t1_weight": gaussian(streams_of[2], (3, C1, C1), (3 * C1) ** -0.5, 0.3125),
        "r1_weight": gaussian(streams_of[3], (2, 2, C1, C2), (4 * C1) ** -0.5, 0.25),
        "s2_weight": gaussian(streams_of[4], (3, 3, C2, C2), (9 * C2) ** -0.5, 0.125),
        "t2_weight": gaussian(streams_of[5], (3, C2, C2), (3 * C2) ** -0.5, 0.21875),
        "r2_weight": gaussian(streams_of[6], (2, 2, C2, C3), (4 * C2) ** -0.5, 0.1875),
        "attn_gain": jnp.clip(1.0 + 0.1 * jax.random.normal(streams_of[7], (C3,), jnp.float32), 0.5, 1.5).astype(jnp.bfloat16),
        "w_query": draw_w_query(jax.random.fold_in(streams_of[12], 71), part),
        "w_key": draw_w_key(jax.random.fold_in(streams_of[12], 71), part),
        "w_value": gaussian(streams_of[10], (C3, C3), C3 ** -0.5, 0.25),
        "w_out": gaussian(streams_of[11], (C3, C3), (C3 // 16) ** -0.5, 1.0),
    }


def spatial(volume, weight):
    row_count = volume.shape[1]
    col_count = volume.shape[2]
    padded = jnp.pad(volume.astype(jnp.float32), ((0, 0), (1, 1), (1, 1), (0, 0)))
    kernel = weight.astype(jnp.float32)
    summed = None
    for tap_row in range(3):
        for tap_col in range(3):
            tap_term = jnp.einsum('tywc,co->tywo', padded[:, tap_row:tap_row + row_count, tap_col:tap_col + col_count], kernel[tap_row, tap_col], precision=lax.Precision.HIGHEST)
            summed = tap_term if summed is None else summed + tap_term
    return summed

def temporal(volume, weight):
    frame_count = volume.shape[0]
    padded = jnp.pad(volume.astype(jnp.float32), ((2, 0), (0, 0), (0, 0), (0, 0)))
    kernel = weight.astype(jnp.float32)
    summed = None
    for tap_time in range(3):
        tap_term = jnp.einsum('tywc,co->tywo', padded[tap_time:tap_time + frame_count], kernel[tap_time], precision=lax.Precision.HIGHEST)
        summed = tap_term if summed is None else summed + tap_term
    return summed

def reduce_pairs(volume, weight):
    frame_count, row_count, col_count, channels = volume.shape
    grouped = volume.astype(jnp.float32).reshape(frame_count, row_count // 2, 2, col_count // 2, 2, channels)
    return jnp.einsum('tyixjc,ijco->tyxo', grouped, weight.astype(jnp.float32), precision=lax.Precision.HIGHEST)

def reference(video, s1_weight, t1_weight, r1_weight, s2_weight, t2_weight, r2_weight, attn_gain, w_query, w_key, w_value, w_out):
    a_first = spatial(video, s1_weight).astype(jnp.bfloat16)
    h_first = jax.nn.silu(temporal(a_first, t1_weight)).astype(jnp.bfloat16)
    d_first = reduce_pairs(h_first, r1_weight).astype(jnp.bfloat16)
    a_second = spatial(d_first, s2_weight).astype(jnp.bfloat16)
    h_second = (d_first.astype(jnp.float32) + jax.nn.silu(temporal(a_second, t2_weight))).astype(jnp.bfloat16)
    h_third = reduce_pairs(h_second, r2_weight).astype(jnp.bfloat16)
    frame_count, row_count, col_count, channels = h_third.shape
    flat = h_third.reshape(frame_count, row_count * col_count, channels)
    score_scale = 1.0 / math.sqrt(channels)

    def attend(sites):
        residual = sites.astype(jnp.float32)
        mean_square = lax.optimization_barrier(jnp.mean(residual * residual, axis=-1, keepdims=True))
        inverse_norm = lax.rsqrt(mean_square + 1e-06)
        normed = (residual * inverse_norm * attn_gain.astype(jnp.float32)).astype(jnp.bfloat16)
        queries = jnp.dot(normed, w_query, preferred_element_type=jnp.float32).astype(jnp.bfloat16)
        key_rows = jnp.dot(normed, w_key, preferred_element_type=jnp.float32).astype(jnp.bfloat16)
        value_rows = jnp.dot(normed, w_value, preferred_element_type=jnp.float32).astype(jnp.bfloat16)
        scores = jnp.dot(queries, key_rows.T, preferred_element_type=jnp.float32) * score_scale
        top_score = lax.optimization_barrier(jnp.max(scores, axis=-1, keepdims=True))
        weights = jnp.exp(scores - top_score)
        totals = lax.optimization_barrier(jnp.sum(weights, axis=-1, keepdims=True))
        attended = (jnp.dot(weights.astype(jnp.bfloat16), value_rows, preferred_element_type=jnp.float32) / totals).astype(jnp.bfloat16)
        return (residual + jnp.dot(attended, w_out, preferred_element_type=jnp.float32)).astype(jnp.bfloat16)
    encoded = lax.map(attend, flat)
    return encoded.reshape(frame_count, row_count, col_count, channels)
```

```python
import math

import jax
import jax.numpy as jnp
from jax import lax
from jax.sharding import PartitionSpec as P


def pair_halo(block, axis, dim, width):
    count = lax.axis_size(axis)
    parity = lax.axis_index(axis) % 2
    top = lax.slice_in_dim(block, 0, width, axis=dim)
    low = lax.slice_in_dim(block, block.shape[dim] - width, None, axis=dim)
    inner = [(i, i ^ 1) for i in range(count)]
    outer = [(i, i + 1) for i in range(1, count - 1, 2)]
    outer = outer + [(target, source) for source, target in outer]
    is_even = parity == 0
    far = lax.ppermute(jnp.where(is_even, top, low), axis, outer)
    near = lax.ppermute(jnp.where(is_even, low, top), axis, inner)
    above = jnp.where(is_even, far, near)
    below = jnp.where(is_even, near, far)
    return jnp.concatenate([above, block, below], axis=dim)


def spatial(volume, weight):
    row_count = volume.shape[1] - 2
    col_count = volume.shape[2]
    padded = jnp.pad(volume, ((0, 0), (0, 0), (1, 1), (0, 0)))
    summed = None
    for tap_row in range(3):
        for tap_col in range(3):
            tap_term = jnp.einsum(
                "tywc,co->tywo",
                padded[:, tap_row : tap_row + row_count, tap_col : tap_col + col_count],
                weight[tap_row, tap_col],
                preferred_element_type=jnp.float32,
            )
            summed = tap_term if summed is None else summed + tap_term
    return summed


def temporal(volume, weight):
    frame_count = volume.shape[0]
    padded = jnp.pad(volume, ((2, 0), (0, 0), (0, 0), (0, 0)))
    summed = None
    for tap_time in range(3):
        tap_term = jnp.einsum(
            "tywc,co->tywo",
            padded[tap_time : tap_time + frame_count],
            weight[tap_time],
            preferred_element_type=jnp.float32,
        )
        summed = tap_term if summed is None else summed + tap_term
    return summed


def reduce_pairs(volume, weight):
    frame_count, row_count, col_count, channels = volume.shape
    grouped = volume.reshape(frame_count, row_count // 2, 2, col_count // 2, 2, channels)
    return jnp.einsum("tyixjc,ijco->tyxo", grouped, weight, preferred_element_type=jnp.float32)


def project(normed, weight):
    return jnp.einsum("...c,co->...o", normed, weight, preferred_element_type=jnp.float32).astype(
        jnp.bfloat16
    )


def frame_attention(own, sites, w_query, w_key, w_value, w_out, score_scale):
    queries = project(own, w_query)
    mapped = jnp.einsum(
        "qc,dc->qd", queries, w_key, preferred_element_type=jnp.float32
    ).astype(jnp.bfloat16)
    scores = (
        jnp.einsum("qc,kc->qk", mapped, sites, preferred_element_type=jnp.float32) * score_scale
    )
    top_score = jnp.max(scores, axis=-1, keepdims=True)
    weights = jnp.exp(scores - top_score)
    totals = jnp.sum(weights, axis=-1, keepdims=True)
    mixed = (
        jnp.einsum(
            "qk,kc->qc", weights.astype(jnp.bfloat16), sites, preferred_element_type=jnp.float32
        )
        / totals
    ).astype(jnp.bfloat16)
    return project(project(mixed, w_value), w_out)


def per_device(
    video,
    s1_weight,
    t1_weight,
    r1_weight,
    s2_weight,
    t2_weight,
    r2_weight,
    attn_gain,
    w_query,
    w_key,
    w_value,
    w_out,
):
    video_rows = pair_halo(video, "ha", 1, 1)
    a_first = spatial(video_rows, s1_weight).astype(jnp.bfloat16)
    h_first = jax.nn.silu(temporal(a_first, t1_weight)).astype(jnp.bfloat16)
    d_first = reduce_pairs(h_first, r1_weight).astype(jnp.bfloat16)
    middle_halo = pair_halo(d_first, "ha", 1, 1)
    a_second = spatial(middle_halo, s2_weight).astype(jnp.bfloat16)
    h_second = (d_first.astype(jnp.float32) + jax.nn.silu(temporal(a_second, t2_weight))).astype(
        jnp.bfloat16
    )
    h_third = reduce_pairs(h_second, r2_weight).astype(jnp.bfloat16)
    frame_count, row_count, col_count, channels = h_third.shape
    score_scale = 1.0 / math.sqrt(channels)
    residual = h_third.astype(jnp.float32)
    mean_square = jnp.mean(residual * residual, axis=-1, keepdims=True)
    inverse_norm = lax.rsqrt(mean_square + 1e-06)
    normed = (residual * inverse_norm * attn_gain.astype(jnp.float32)).astype(jnp.bfloat16)
    device_count = lax.axis_size("ha")
    group_size = device_count // frame_count
    own_frame = lax.axis_index("ha") // group_size
    steps = range(frame_count)
    flat = normed.reshape(frame_count, row_count * col_count, channels)
    turns = [
        [(d, (d // group_size ^ k) * group_size + d % group_size) for d in range(device_count)]
        for k in steps
    ]
    picked = [lax.dynamic_index_in_dim(flat, own_frame ^ k, 0, keepdims=False) for k in steps]
    own = jnp.concatenate(
        [picked[0]] + [lax.ppermute(picked[k], "ha", turns[k]) for k in steps if k], axis=0
    )
    sites = own
    bit = group_size // 2
    while bit:
        sites = jnp.concatenate(
            [sites, lax.ppermute(sites, "ha", [(d, d ^ bit) for d in range(device_count)])], axis=0
        )
        bit //= 2
    mixed = frame_attention(own, sites, w_query, w_key, w_value, w_out, score_scale)
    mixed = mixed.reshape(frame_count, row_count * col_count, channels)
    back = jnp.stack([mixed[0]] + [lax.ppermute(mixed[k], "ha", turns[k]) for k in steps if k])
    back = jnp.stack(
        [lax.dynamic_index_in_dim(back, own_frame ^ t, 0, keepdims=False) for t in steps]
    )
    encoded = residual + back.reshape(residual.shape).astype(jnp.float32)
    return encoded.astype(jnp.bfloat16)


def solution(mesh):
    placed = (P("groups", "ha", None, None), P(), P(), P(), P(), P(), P(), P(), P(), P(), P(), P())
    return jax.shard_map(
        per_device,
        mesh=mesh,
        in_specs=placed,
        out_specs=P("groups", "ha", None, None),
        check_vma=False,
    )
```

```python
import functools
import math

import jax
import jax.numpy as jnp
from jax import lax
from jax.experimental import pallas as pl
from jax.experimental.pallas import tpu as pltpu
from jax.sharding import PartitionSpec as P

F32 = jnp.float32
BF16 = jnp.bfloat16
AXIS = "ha"
PHASES = 4


def dot(left, right):
    return jnp.dot(left, right, preferred_element_type=F32)


def lanes(parts):
    return parts[0] if len(parts) == 1 else jnp.concatenate(parts, axis=-1)


def silu(x):
    return 0.5 * x * (1.0 + jnp.tanh(0.5 * x))


def shifted(x, step, period):
    rows = x.shape[0]
    place = lax.broadcasted_iota(jnp.int32, x.shape, 0) % period
    moved = pltpu.roll(x, step % rows, 0)
    return jnp.where(place == (0 if step == 1 else period - 1), 0.0, moved)


def place_phases(total, tap_ref, out_of):
    _, frames, cols, channels = tap_ref.shape
    count = cols // PHASES
    for tap in range(3):
        tap_ref[tap] = total[:, tap * channels : (tap + 1) * channels].reshape(
            frames, cols, channels
        )
    for frame in range(frames):
        def strided(tap, phase):
            return tap_ref[tap, frame, pl.ds(phase, count, stride=PHASES), :]

        for phase in range(PHASES):
            before = (
                shifted(strided(0, PHASES - 1), 1, count)
                if phase == 0
                else strided(0, phase - 1)
            )
            after = (
                shifted(strided(2, 0), -1, count)
                if phase == PHASES - 1
                else strided(2, phase + 1)
            )
            out_of(frame, phase, before + strided(1, phase) + after)


def tap_matrix(w_ref, row):
    return lanes([w_ref[row, tap] for tap in range(3)])


def edge_kernel(video_ref, w_ref, far_ref, near_ref, tap_ref):
    parity = lax.axis_index(AXIS) % 2
    frames, rows, cols, channels = video_ref.shape
    for ref, side in ((far_ref, parity), (near_ref, 1 - parity)):
        row = side * (rows - 1)
        weight = tap_matrix(w_ref, 2 - 2 * side)
        total = dot(video_ref[:, row].reshape(frames * cols, channels), weight)

        def store(frame, phase, value, ref=ref):
            ref[frame, phase] = value.astype(BF16)

        place_phases(total, tap_ref, store)


def inner_kernel(video_ref, w_ref, acc_ref, tap_ref):
    frames, rows, cols, channels = video_ref.shape
    for row in range(rows):
        total = None
        for tap in range(3):
            source = row + tap - 1
            if 0 <= source < rows:
                term = dot(
                    video_ref[:, source].reshape(frames * cols, channels), tap_matrix(w_ref, tap)
                )
                total = term if total is None else total + term

        def store(frame, phase, value, row=row):
            acc_ref[frame, row, phase] = value

        place_phases(total, tap_ref, store)


def first_kernel(acc_ref, far_ref, near_ref, t_ref, r_ref, d_ref, far_out, near_out, a_ref, h_ref):
    frames, rows, phases, count, channels = acc_ref.shape
    parity = lax.axis_index(AXIS) % 2
    is_even = parity == 0
    sites = rows * phases * count
    for frame in range(frames):
        far = far_ref[frame].astype(F32)
        near = near_ref[frame].astype(F32)
        above = jnp.where(is_even, far, near)
        below = jnp.where(is_even, near, far)
        for row in range(rows):
            value = acc_ref[frame, row]
            if row == 0:
                value = value + above
            if row == rows - 1:
                value = value + below
            a_ref[frame, row] = value.astype(BF16)
        taps = range(max(0, 2 - frame), 3)
        left = lanes([a_ref[frame + tap - 2].reshape(sites, channels) for tap in taps])
        weight = jnp.concatenate([t_ref[tap] for tap in taps], axis=0) if len(taps) > 1 else t_ref[2]
        h_ref[frame] = silu(dot(left, weight)).astype(BF16).reshape(h_ref.shape[1:])
    wide = r_ref.shape[-1]
    weight = r_ref[...].reshape(4 * channels, wide)
    for out_row in range(rows // 2):
        for side in range(phases // 2):
            left = lanes(
                [
                    h_ref[:, 2 * out_row + i, 2 * side + j].reshape(frames * count, channels)
                    for i in range(2)
                    for j in range(2)
                ]
            )
            value = dot(left, weight).astype(BF16).reshape(frames, count, wide)
            d_ref[:, out_row, side] = value
    last = rows // 2 - 1
    far_out[...] = d_ref[:, parity * last]
    near_out[...] = d_ref[:, (1 - parity) * last]


def place_pairs(total, sites, count, channels):
    even, odd = total[:sites], total[sites:]
    first, middle, last = (slice(tap * channels, (tap + 1) * channels) for tap in range(3))
    return (
        shifted(odd[:, first], 1, count) + even[:, middle] + odd[:, last],
        even[:, first] + odd[:, middle] + shifted(even[:, last], -1, count),
    )


def side_rows(ref, row):
    frames, _, sides, count, channels = ref.shape
    return jnp.concatenate(
        [ref[:, row, side].reshape(frames * count, channels) for side in range(sides)], axis=0
    )


def middle_kernel(d_ref, w_ref, acc_ref):
    frames, rows, sides, count, channels = d_ref.shape
    sites = frames * count
    for row in range(rows):
        total = None
        for tap in range(3):
            source = row + tap - 1
            if 0 <= source < rows:
                term = dot(side_rows(d_ref, source), tap_matrix(w_ref, tap))
                total = term if total is None else total + term
        for side, value in enumerate(place_pairs(total, sites, count, channels)):
            acc_ref[:, row, side] = value.reshape(frames, count, channels)


def second_kernel(
    acc_ref, far_ref, near_ref, d_ref, w_ref, t_ref, r_ref, gain_ref, *refs, group_size
):
    frames, rows, sides, count, channels = d_ref.shape
    h_out, *blocks = refs[: frames + 1]
    a_ref, h_ref = refs[frames + 1 :]
    index = lax.axis_index(AXIS)
    parity = index % 2
    is_even = parity == 0
    sites = frames * count
    halos = []
    for side in range(2):
        far = far_ref[:, side].reshape(sites, channels)
        near = near_ref[:, side].reshape(sites, channels)
        halos.append((far, near))
    far = jnp.concatenate([pair[0] for pair in halos], axis=0)
    near = jnp.concatenate([pair[1] for pair in halos], axis=0)
    above = jnp.where(is_even, far, near)
    below = jnp.where(is_even, near, far)
    for row in range(rows):
        values = [acc_ref[:, row, side].reshape(sites, channels) for side in range(sides)]
        for here, halo, tap in ((0, above, 0), (rows - 1, below, 2)):
            if row == here:
                more = place_pairs(dot(halo, tap_matrix(w_ref, tap)), sites, count, channels)
                values = [value + extra for value, extra in zip(values, more)]
        for side, value in enumerate(values):
            a_ref[:, row, side] = value.astype(BF16).reshape(frames, count, channels)
    frame_sites = rows * sides * count
    for frame in range(frames):
        taps = range(max(0, 2 - frame), 3)
        left = lanes([a_ref[frame + tap - 2].reshape(frame_sites, channels) for tap in taps])
        weight = jnp.concatenate([t_ref[tap] for tap in taps], axis=0) if len(taps) > 1 else t_ref[2]
        value = d_ref[frame].reshape(frame_sites, channels).astype(F32) + silu(dot(left, weight))
        h_ref[frame] = value.astype(BF16).reshape(h_ref.shape[1:])
    wide = r_ref.shape[-1]
    weight = r_ref[...].reshape(4 * channels, wide)
    gain = gain_ref[...].astype(F32)
    place = index // group_size
    for out_row in range(rows // 2):
        left = lanes(
            [
                h_ref[:, 2 * out_row + i, j].reshape(sites, channels)
                for i in range(2)
                for j in range(2)
            ]
        )
        residual = dot(left, weight).astype(BF16)
        h_out[:, out_row] = residual.reshape(frames, count, wide)
        residual = residual.astype(F32)
        mean_square = jnp.mean(residual * residual, axis=-1, keepdims=True)
        normed = (residual * lax.rsqrt(mean_square + 1e-06) * gain).astype(BF16)
        a_ref_shape = (frames, count, wide)
        refs_normed = normed.reshape(a_ref_shape)
        for frame in range(frames):
            for step, block in enumerate(blocks):

                @pl.when(place ^ step == frame)
                def _(block=block, frame=frame, out_row=out_row):
                    block[pl.ds(out_row * count, count), :] = refs_normed[frame]


def query_kernel(own_ref, q_ref, k_ref, out_ref):
    queries = dot(own_ref[...], q_ref[...]).astype(BF16)
    out_ref[...] = lax.dot_general(
        queries, k_ref[...], (((1,), (1,)), ((), ())), preferred_element_type=F32
    ).astype(BF16)


def attention_kernel(mapped_ref, sites_ref, v_ref, o_ref, *blocks):
    channels = mapped_ref.shape[-1]
    score_scale = 1.0 / math.sqrt(channels)
    scores = (
        lax.dot_general(
            mapped_ref[...], sites_ref[...], (((1,), (1,)), ((), ())), preferred_element_type=F32
        )
        * score_scale
    )
    weights = jnp.exp(scores - jnp.max(scores, axis=-1, keepdims=True))
    totals = jnp.sum(weights, axis=-1, keepdims=True)
    mixed = (dot(weights.astype(BF16), sites_ref[...]) / totals).astype(BF16)
    attended = dot(mixed, v_ref[...]).astype(BF16)
    result = dot(attended, o_ref[...]).astype(BF16)
    count = blocks[0].shape[0]
    for step, block in enumerate(blocks):
        block[...] = result[step * count : (step + 1) * count]


def sum_kernel(h_ref, *refs, group_size):
    *blocks, out_ref = refs
    frames, rows, count, channels = h_ref.shape
    place = lax.axis_index(AXIS) // group_size
    for step, block in enumerate(blocks):
        frame = place ^ step
        value = block[...].astype(F32).reshape(rows, count, channels)
        out_ref[frame] = (h_ref[frame].astype(F32) + value).astype(BF16)


def call(kernel, outs, scratch, args, flops, name):
    vmem = pl.BlockSpec(memory_space=pltpu.VMEM)
    shapes = [jax.ShapeDtypeStruct(shape, dtype) for shape, dtype in outs]
    moved = sum(math.prod(arg.shape) * arg.dtype.itemsize for arg in args)
    moved += sum(math.prod(shape) * jnp.dtype(dtype).itemsize for shape, dtype in outs)
    used = moved + sum(
        math.prod(shape) * jnp.dtype(dtype).itemsize for shape, dtype in scratch
    )
    return pl.pallas_call(
        kernel,
        out_shape=shapes,
        in_specs=[vmem] * len(args),
        out_specs=[vmem] * len(outs),
        scratch_shapes=[pltpu.VMEM(shape, dtype) for shape, dtype in scratch],
        compiler_params=pltpu.CompilerParams(vmem_limit_bytes=LIMIT),
        cost_estimate=pl.CostEstimate(flops=int(flops), bytes_accessed=int(moved), transcendentals=0),
        name=name,
    )(*args)


LIMIT = 40 * 1024 * 1024


def per_device(
    video,
    s1_weight,
    t1_weight,
    r1_weight,
    s2_weight,
    t2_weight,
    r2_weight,
    attn_gain,
    w_query,
    w_key,
    w_value,
    w_out,
):
    frames, rows, cols, c0 = video.shape
    c1, c2, c3 = s1_weight.shape[-1], s2_weight.shape[-1], w_out.shape[-1]
    count = cols // PHASES
    devices = lax.axis_size(AXIS)
    group_size = devices // frames
    inner = [(d, d ^ 1) for d in range(devices)]
    outer = [(d, d + 1) for d in range(1, devices - 1, 2)]
    outer = outer + [(target, source) for source, target in outer]
    turns = [
        [(d, (d // group_size ^ k) * group_size + d % group_size) for d in range(devices)]
        for k in range(frames)
    ]

    edge = ((frames, PHASES, count, c1), BF16)
    taps = ((3, frames, cols, c1), F32)
    site_flops = 2 * frames * cols * 3 * c0 * c1
    far, near = call(edge_kernel, [edge, edge], [taps], [video, s1_weight], 2 * site_flops, "edge")
    far = lax.ppermute(far, AXIS, outer)
    near = lax.ppermute(near, AXIS, inner)
    shape = (frames, rows, PHASES, count, c1)
    (acc,) = call(
        inner_kernel, [(shape, F32)], [taps], [video, s1_weight], 10 * site_flops, "inner"
    )
    half = (frames, rows // 2, 2, count, c2)
    edge = ((frames, 2, count, c2), BF16)
    d_first, far, near = call(
        first_kernel,
        [(half, BF16), edge, edge],
        [(shape, BF16), (shape, BF16)],
        [acc, far, near, t1_weight, r1_weight],
        5e8,
        "first",
    )
    far = lax.ppermute(far, AXIS, outer)
    near = lax.ppermute(near, AXIS, inner)
    (acc,) = call(middle_kernel, [(half, F32)], [], [d_first, s2_weight], 6e8, "middle")
    site_rows = rows // 4
    block = ((site_rows * count, c3), BF16)
    residual, *blocks = call(
        functools.partial(second_kernel, group_size=group_size),
        [((frames, site_rows, count, c3), BF16)] + [block] * frames,
        [(half, BF16), (half, BF16)],
        [acc, far, near, d_first, s2_weight, t2_weight, r2_weight, attn_gain.reshape(1, c3)],
        8e8,
        "second",
    )
    own = jnp.concatenate(
        [blocks[0]] + [lax.ppermute(blocks[k], AXIS, turns[k]) for k in range(1, frames)], axis=0
    )
    sites = own
    bit = group_size // 2
    while bit:
        sites = jnp.concatenate(
            [sites, lax.ppermute(sites, AXIS, [(d, d ^ bit) for d in range(devices)])], axis=0
        )
        bit //= 2
    (mapped,) = call(query_kernel, [(own.shape, BF16)], [], [own, w_query, w_key], 2e8, "query")
    blocks = call(
        attention_kernel, [block] * frames, [], [mapped, sites, w_value, w_out], 6e8, "attention"
    )
    blocks = [blocks[0]] + [lax.ppermute(blocks[k], AXIS, turns[k]) for k in range(1, frames)]
    (encoded,) = call(
        functools.partial(sum_kernel, group_size=group_size),
        [(residual.shape, BF16)],
        [],
        [residual, *blocks],
        1e6,
        "sum",
    )
    return encoded


def solution(mesh):
    placed = (P("groups", "ha", None, None), P(), P(), P(), P(), P(), P(), P(), P(), P(), P(), P())
    return jax.shard_map(
        per_device,
        mesh=mesh,
        in_specs=placed,
        out_specs=P("groups", "ha", None, None),
        check_vma=False,
    )
```

```python
import functools
import math

import jax
import jax.numpy as jnp
from jax import lax
from jax.experimental import pallas as pl
from jax.experimental.pallas import tpu as pltpu
from jax.sharding import PartitionSpec as P

F32 = jnp.float32
BF16 = jnp.bfloat16
AXIS = "ha"
BOTH = ("groups", AXIS)
PHASES = 4


def dot(left, right):
    return jnp.dot(left, right, preferred_element_type=F32)


def neighbours(far, near):
    index = lax.axis_index(AXIS)
    is_even = index % 2 == 0
    above = jnp.where(is_even, far, near)
    below = jnp.where(is_even, near, far)
    zero = jnp.zeros_like(above)
    return (
        jnp.where(index == 0, zero, above),
        jnp.where(index == lax.axis_size(AXIS) - 1, zero, below),
    )


def lanes(parts):
    return parts[0] if len(parts) == 1 else jnp.concatenate(parts, axis=-1)


def silu(x):
    return 0.5 * x * (1.0 + jnp.tanh(0.5 * x))


def shifted(x, step, period):
    rows = x.shape[0]
    place = lax.broadcasted_iota(jnp.int32, x.shape, 0) % period
    moved = pltpu.roll(x, step % rows, 0)
    return jnp.where(place == (0 if step == 1 else period - 1), 0.0, moved)


def place_phases(total, tap_ref, out_of):
    _, frames, cols, channels = tap_ref.shape
    count = cols // PHASES
    for tap in range(3):
        tap_ref[tap] = total[:, tap * channels : (tap + 1) * channels].reshape(
            frames, cols, channels
        )
    for frame in range(frames):
        def strided(tap, phase):
            return tap_ref[tap, frame, pl.ds(phase, count, stride=PHASES), :]

        for phase in range(PHASES):
            before = (
                shifted(strided(0, PHASES - 1), 1, count)
                if phase == 0
                else strided(0, phase - 1)
            )
            after = (
                shifted(strided(2, 0), -1, count)
                if phase == PHASES - 1
                else strided(2, phase + 1)
            )
            out_of(frame, phase, before + strided(1, phase) + after)


def tap_matrix(w_ref, row):
    return lanes([w_ref[row, tap] for tap in range(3)])


def edge_kernel(video_ref, w_ref, far_ref, near_ref, row_ref, weight_ref, tap_ref, row_sem, weight_sem):
    parity = lax.axis_index(AXIS) % 2
    frames, rows, cols, channels = video_ref.shape
    sides = (parity, 1 - parity)
    copies = []
    for at, side in enumerate(sides):
        pair = (
            pltpu.make_async_copy(
                video_ref.at[:, side * (rows - 1)], row_ref.at[at], row_sem.at[at]
            ),
            pltpu.make_async_copy(w_ref.at[2 - 2 * side], weight_ref.at[at], weight_sem.at[at]),
        )
        for copy in pair:
            copy.start()
        copies.append(pair)
    for at, ref in enumerate((far_ref, near_ref)):
        for copy in copies[at]:
            copy.wait()
        total = dot(row_ref[at].reshape(frames * cols, channels), tap_matrix(weight_ref, at))

        def store(frame, phase, value, ref=ref):
            ref[frame, phase] = value.astype(BF16)

        place_phases(total, tap_ref, store)


def inner_kernel(video_ref, w_ref, acc_ref, tap_ref):
    frames, rows, cols, channels = video_ref.shape
    for row in range(rows):
        total = None
        for tap in range(3):
            source = row + tap - 1
            if 0 <= source < rows:
                term = dot(
                    video_ref[:, source].reshape(frames * cols, channels), tap_matrix(w_ref, tap)
                )
                total = term if total is None else total + term

        def store(frame, phase, value, row=row):
            acc_ref[frame, row, phase] = value

        place_phases(total, tap_ref, store)


def first_kernel(acc_ref, far_ref, near_ref, t_ref, r_ref, d_ref, far_out, near_out, a_ref, h_ref):
    frames, rows, phases, count, channels = acc_ref.shape
    parity = lax.axis_index(AXIS) % 2
    sites = rows * phases * count
    for frame in range(frames):
        far = far_ref[frame].astype(F32)
        near = near_ref[frame].astype(F32)
        above, below = neighbours(far, near)
        for row in range(rows):
            value = acc_ref[frame, row]
            if row == 0:
                value = value + above
            if row == rows - 1:
                value = value + below
            a_ref[frame, row] = value.astype(BF16)
        taps = range(max(0, 2 - frame), 3)
        left = lanes([a_ref[frame + tap - 2].reshape(sites, channels) for tap in taps])
        weight = jnp.concatenate([t_ref[tap] for tap in taps], axis=0) if len(taps) > 1 else t_ref[2]
        h_ref[frame] = silu(dot(left, weight)).astype(BF16).reshape(h_ref.shape[1:])
    wide = r_ref.shape[-1]
    weight = r_ref[...].reshape(4 * channels, wide)
    for out_row in range(rows // 2):
        for side in range(phases // 2):
            left = lanes(
                [
                    h_ref[:, 2 * out_row + i, 2 * side + j].reshape(frames * count, channels)
                    for i in range(2)
                    for j in range(2)
                ]
            )
            value = dot(left, weight).astype(BF16).reshape(frames, count, wide)
            d_ref[:, out_row, side] = value
    last = rows // 2 - 1
    far_out[...] = d_ref[:, parity * last]
    near_out[...] = d_ref[:, (1 - parity) * last]


def place_pairs(total, sites, count, channels):
    even, odd = total[:sites], total[sites:]
    first, middle, last = (slice(tap * channels, (tap + 1) * channels) for tap in range(3))
    return (
        shifted(odd[:, first], 1, count) + even[:, middle] + odd[:, last],
        even[:, first] + odd[:, middle] + shifted(even[:, last], -1, count),
    )


def side_rows(ref, row):
    frames, _, sides, count, channels = ref.shape
    return jnp.concatenate(
        [ref[:, row, side].reshape(frames * count, channels) for side in range(sides)], axis=0
    )


def middle_kernel(d_ref, w_ref, acc_ref):
    frames, rows, sides, count, channels = d_ref.shape
    sites = frames * count
    for row in range(rows):
        total = None
        for tap in range(3):
            source = row + tap - 1
            if 0 <= source < rows:
                term = dot(side_rows(d_ref, source), tap_matrix(w_ref, tap))
                total = term if total is None else total + term
        for side, value in enumerate(place_pairs(total, sites, count, channels)):
            acc_ref[:, row, side] = value.reshape(frames, count, channels)


def second_kernel(
    acc_ref, far_ref, near_ref, d_ref, w_ref, t_ref, r_ref, gain_ref, *refs, group_size
):
    frames, rows, sides, count, channels = d_ref.shape
    h_out, *blocks = refs[: frames + 1]
    a_ref, h_ref = refs[frames + 1 :]
    index = lax.axis_index(AXIS)
    sites = frames * count
    halos = []
    for side in range(2):
        far = far_ref[:, side].reshape(sites, channels)
        near = near_ref[:, side].reshape(sites, channels)
        halos.append((far, near))
    far = jnp.concatenate([pair[0] for pair in halos], axis=0)
    near = jnp.concatenate([pair[1] for pair in halos], axis=0)
    above, below = neighbours(far, near)
    for row in range(rows):
        values = [acc_ref[:, row, side].reshape(sites, channels) for side in range(sides)]
        for here, halo, tap in ((0, above, 0), (rows - 1, below, 2)):
            if row == here:
                more = place_pairs(dot(halo, tap_matrix(w_ref, tap)), sites, count, channels)
                values = [value + extra for value, extra in zip(values, more)]
        for side, value in enumerate(values):
            a_ref[:, row, side] = value.astype(BF16).reshape(frames, count, channels)
    frame_sites = rows * sides * count
    for frame in range(frames):
        taps = range(max(0, 2 - frame), 3)
        left = lanes([a_ref[frame + tap - 2].reshape(frame_sites, channels) for tap in taps])
        weight = jnp.concatenate([t_ref[tap] for tap in taps], axis=0) if len(taps) > 1 else t_ref[2]
        value = d_ref[frame].reshape(frame_sites, channels).astype(F32) + silu(dot(left, weight))
        h_ref[frame] = value.astype(BF16).reshape(h_ref.shape[1:])
    wide = r_ref.shape[-1]
    weight = r_ref[...].reshape(4 * channels, wide)
    gain = gain_ref[...].astype(F32)
    place = index // group_size
    for out_row in range(rows // 2):
        left = lanes(
            [
                h_ref[:, 2 * out_row + i, j].reshape(sites, channels)
                for i in range(2)
                for j in range(2)
            ]
        )
        residual = dot(left, weight).astype(BF16)
        h_out[:, out_row] = residual.reshape(frames, count, wide)
        residual = residual.astype(F32)
        mean_square = jnp.mean(residual * residual, axis=-1, keepdims=True)
        normed = (residual * lax.rsqrt(mean_square + 1e-06) * gain).astype(BF16)
        a_ref_shape = (frames, count, wide)
        refs_normed = normed.reshape(a_ref_shape)
        for frame in range(frames):
            for step, block in enumerate(blocks):

                @pl.when(place ^ step == frame)
                def _(block=block, frame=frame, out_row=out_row):
                    block[pl.ds(out_row * count, count), :] = refs_normed[frame]


def scored(mapped, sites):
    scores = lax.dot_general(
        mapped, sites, (((1,), (1,)), ((), ())), preferred_element_type=F32
    ) * (1.0 / math.sqrt(mapped.shape[-1]))
    top = jnp.max(scores, axis=-1, keepdims=True)
    weights = jnp.exp(scores - top)
    return top, jnp.sum(weights, axis=-1, keepdims=True), dot(weights.astype(BF16), sites)


def joined(left, right):
    top = jnp.maximum(left[0], right[0])
    one, two = jnp.exp(left[0] - top), jnp.exp(right[0] - top)
    return top, left[1] * one + right[1] * two, left[2] * one + right[2] * two


def query_kernel(own_ref, q_ref, k_ref, out_ref):
    queries = dot(own_ref[...], q_ref[...]).astype(BF16)
    out_ref[...] = lax.dot_general(
        queries, k_ref[...], (((1,), (1,)), ((), ())), preferred_element_type=F32
    ).astype(BF16)


def early_kernel(mapped_ref, *refs):
    *site_refs, top_ref, total_ref, mixed_ref = refs
    sites = jnp.concatenate([ref[...] for ref in site_refs], axis=0)
    top, total, mixed_ref[...] = scored(mapped_ref[...], sites)
    top_ref[...] = jnp.broadcast_to(top, top_ref.shape)
    total_ref[...] = jnp.broadcast_to(total, total_ref.shape)


def late_kernel(mapped_ref, top_ref, total_ref, mixed_ref, v_ref, o_ref, *refs, parts):
    site_refs, blocks = refs[:parts], refs[parts:]
    sites = jnp.concatenate([ref[...] for ref in site_refs], axis=0)
    early = top_ref[:, :1], total_ref[:, :1], mixed_ref[...]
    _, total, mixed = joined(early, scored(mapped_ref[...], sites))
    attended = dot((mixed / total).astype(BF16), v_ref[...]).astype(BF16)
    result = dot(attended, o_ref[...]).astype(BF16)
    count = blocks[0].shape[0]
    for step, block in enumerate(blocks):
        block[...] = result[step * count : (step + 1) * count]


def sum_kernel(h_ref, *refs, group_size):
    *blocks, out_ref = refs
    frames, rows, count, channels = h_ref.shape
    place = lax.axis_index(AXIS) // group_size
    for step, block in enumerate(blocks):
        frame = place ^ step
        value = block[...].astype(F32).reshape(rows, count, channels)
        out_ref[frame] = (h_ref[frame].astype(F32) + value).astype(BF16)


def call(kernel, outs, scratch, args, flops, name, space=pltpu.VMEM, sems=(), limit=None):
    vmem = pl.BlockSpec(memory_space=pltpu.VMEM)
    shapes = [jax.ShapeDtypeStruct(shape, dtype) for shape, dtype in outs]
    moved = sum(math.prod(arg.shape) * arg.dtype.itemsize for arg in args)
    moved += sum(math.prod(shape) * jnp.dtype(dtype).itemsize for shape, dtype in outs)
    return pl.pallas_call(
        kernel,
        out_shape=shapes,
        in_specs=[pl.BlockSpec(memory_space=space)] * len(args),
        out_specs=[vmem] * len(outs),
        scratch_shapes=[pltpu.VMEM(shape, dtype) for shape, dtype in scratch] + list(sems),
        compiler_params=pltpu.CompilerParams(vmem_limit_bytes=limit or LIMIT),
        cost_estimate=pl.CostEstimate(flops=int(flops), bytes_accessed=int(moved), transcendentals=0),
        name=name,
    )(*args)


LIMIT = 40 * 1024 * 1024
WHOLE = 67043328


def per_device(
    video,
    s1_weight,
    t1_weight,
    r1_weight,
    s2_weight,
    t2_weight,
    r2_weight,
    attn_gain,
    w_query,
    w_key,
    w_value,
    w_out,
):
    frames, rows, cols, c0 = video.shape
    c1, c2, c3 = s1_weight.shape[-1], s2_weight.shape[-1], w_out.shape[-1]
    count = cols // PHASES
    devices = lax.axis_size(AXIS)
    group_size = devices // frames
    inner = [(d, d ^ 1) for d in range(devices)]
    groups = lax.axis_size("groups")
    outer = [(d, d + 1) for d in range(1, devices - 1, 2)]
    outer = outer + [(target, source) for source, target in outer]
    outer = [(g * devices + a, g * devices + b) for g in range(groups) for a, b in outer]
    if groups % 2 == 0:
        outer += [
            (g * devices + end, (g ^ 1) * devices + end)
            for g in range(groups)
            for end in (0, devices - 1)
        ]
    turns = [
        [(d, (d // group_size ^ k) * group_size + d % group_size) for d in range(devices)]
        for k in range(frames)
    ]

    edge = ((frames, PHASES, count, c1), BF16)
    taps = ((3, frames, cols, c1), F32)
    site_flops = 2 * frames * cols * 3 * c0 * c1
    far, near = call(
        edge_kernel,
        [edge, edge],
        [((2, frames, cols, c0), BF16), ((2, 3, c0, c1), BF16), taps],
        [video, s1_weight],
        2 * site_flops,
        "edge",
        pltpu.HBM,
        [pltpu.SemaphoreType.DMA((2,))] * 2,
        WHOLE,
    )
    far = lax.ppermute(far, BOTH, outer)
    near = lax.ppermute(near, AXIS, inner)
    shape = (frames, rows, PHASES, count, c1)
    (acc,) = call(
        inner_kernel, [(shape, F32)], [taps], [video, s1_weight], 10 * site_flops, "inner"
    )
    half = (frames, rows // 2, 2, count, c2)
    edge = ((frames, 2, count, c2), BF16)
    d_first, far, near = call(
        first_kernel,
        [(half, BF16), edge, edge],
        [(shape, BF16), (shape, BF16)],
        [acc, far, near, t1_weight, r1_weight],
        5e8,
        "first",
    )
    far = lax.ppermute(far, BOTH, outer)
    near = lax.ppermute(near, AXIS, inner)
    (acc,) = call(middle_kernel, [(half, F32)], [], [d_first, s2_weight], 6e8, "middle")
    site_rows = rows // 4
    block = ((site_rows * count, c3), BF16)
    residual, *blocks = call(
        functools.partial(second_kernel, group_size=group_size),
        [((frames, site_rows, count, c3), BF16)] + [block] * frames,
        [(half, BF16), (half, BF16)],
        [acc, far, near, d_first, s2_weight, t2_weight, r2_weight, attn_gain.reshape(1, c3)],
        8e8,
        "second",
    )
    own = jnp.concatenate(
        [blocks[0]] + [lax.ppermute(blocks[k], AXIS, turns[k]) for k in range(1, frames)], axis=0
    )
    site_count = own.shape[0]
    bits = []
    bit = group_size // 2
    while bit > 1:
        bits.append(bit)
        bit //= 2

    def swap(x, bit):
        return lax.ppermute(x, AXIS, [(d, d ^ bit) for d in range(devices)])

    far_sites = []
    have = [own]
    for bit in bits:
        whole = jnp.concatenate(have, axis=0) if len(have) > 1 else have[0]
        got = swap(whole, bit)
        far_sites.append(got)
        have = have + [got]
    partner = swap(own, 1)
    (mapped,) = call(query_kernel, [(own.shape, BF16)], [], [own, w_query, w_key], 2e8, "query")
    stats = ((site_count, 128), F32)
    early = call(
        early_kernel,
        [stats, stats, (own.shape, F32)],
        [],
        [mapped, own, partner],
        3e8,
        "early",
    )
    far_sites = jnp.concatenate(far_sites, axis=0) if len(far_sites) > 1 else far_sites[0]
    far_sites, early = lax.optimization_barrier((far_sites, early))
    late = [far_sites, swap(far_sites, 1)]
    blocks = call(
        functools.partial(late_kernel, parts=len(late)),
        [block] * frames,
        [],
        [mapped, *early, w_value, w_out, *late],
        6e8,
        "late",
    )
    blocks = [blocks[0]] + [lax.ppermute(blocks[k], AXIS, turns[k]) for k in range(1, frames)]
    (encoded,) = call(
        functools.partial(sum_kernel, group_size=group_size),
        [(residual.shape, BF16)],
        [],
        [residual, *blocks],
        1e6,
        "sum",
    )
    return encoded


def solution(mesh):
    placed = (P("groups", "ha", None, None), P(), P(), P(), P(), P(), P(), P(), P(), P(), P(), P())
    return jax.shard_map(
        per_device,
        mesh=mesh,
        in_specs=placed,
        out_specs=P("groups", "ha", None, None),
        check_vma=False,
    )
```

```python
import functools
import math

import jax
import jax.numpy as jnp
from jax import lax
from jax.experimental import pallas as pl
from jax.experimental.pallas import tpu as pltpu
from jax.sharding import PartitionSpec as P


F32 = jnp.float32
BF16 = jnp.bfloat16
AXIS = "ha"
BOTH = ("groups", AXIS)
PHASES = 4


def dot(left, right):
    return jnp.dot(left, right, preferred_element_type=F32)


def turn():
    return lax.axis_index(AXIS) % 2


def whole_row(row, count):
    return row + turn() * (count - 1 - 2 * row)


def inside(far):
    index = lax.axis_index(AXIS)
    at_end = (index == 0) | (index == lax.axis_size(AXIS) - 1)
    return jnp.where(at_end, jnp.zeros_like(far), far)


def causal(a, t_ref):
    frames, sites, channels = a.shape
    total = None
    for lag in range(3):
        count = frames - lag
        term = dot(a[:count].reshape(count * sites, channels), t_ref[2 - lag]).reshape(
            count, sites, -1
        )
        total = (
            term if total is None else jnp.concatenate([total[:lag], total[lag:] + term], axis=0)
        )
    return total


def reduction(r_ref):
    first = turn()
    return jnp.concatenate(
        [r_ref[first, 0], r_ref[first, 1], r_ref[1 - first, 0], r_ref[1 - first, 1]], axis=0
    )


def lanes(parts):
    return parts[0] if len(parts) == 1 else jnp.concatenate(parts, axis=-1)


def silu(x):
    return 0.5 * x * (1.0 + jnp.tanh(0.5 * x))


def shifted(x, step, period):
    rows = x.shape[0]
    place = lax.broadcasted_iota(jnp.int32, x.shape, 0) % period
    moved = pltpu.roll(x, step % rows, 0)
    return jnp.where(place == (0 if step == 1 else period - 1), 0.0, moved)


def place_phases(total, tap_ref, out_of):
    _, frames, cols, channels = tap_ref.shape
    count = cols // PHASES
    for tap in range(3):
        tap_ref[tap] = total[:, tap * channels : (tap + 1) * channels].reshape(
            frames, cols, channels
        )
    for frame in range(frames):
        def strided(tap, phase):
            return tap_ref[tap, frame, pl.ds(phase, count, stride=PHASES), :]

        for phase in range(PHASES):
            before = (
                shifted(strided(0, PHASES - 1), 1, count)
                if phase == 0
                else strided(0, phase - 1)
            )
            after = (
                shifted(strided(2, 0), -1, count)
                if phase == PHASES - 1
                else strided(2, phase + 1)
            )
            out_of(frame, phase, before + strided(1, phase) + after)


def tap_matrix(w_ref, row):
    return lanes([w_ref[row, tap] for tap in range(3)])


def edge_kernel(
    video_ref, w_ref, far_ref, near_ref, row_ref, weight_ref, tap_ref, row_sem, weight_sem
):
    frames, rows, cols, channels = video_ref.shape
    side = turn()
    copies = []
    for at, (row, tap) in enumerate((((rows - 1) * side, 2 - 2 * side), ((rows - 1) * (1 - side), 2 * side))):
        group = [
            pltpu.make_async_copy(
                video_ref.at[frame, row], row_ref.at[at, frame], row_sem.at[at, frame]
            )
            for frame in range(frames)
        ] + [
            pltpu.make_async_copy(
                w_ref.at[tap, column], weight_ref.at[at, column], weight_sem.at[at, column]
            )
            for column in range(3)
        ]
        for copy in group:
            copy.start()
        copies.append(group)
    for at, ref in enumerate((far_ref, near_ref)):
        for copy in copies[at]:
            copy.wait()
        total = dot(row_ref[at].reshape(frames * cols, channels), tap_matrix(weight_ref, at))

        def store(frame, phase, value, ref=ref):
            ref[frame, phase] = value.astype(BF16)

        place_phases(total, tap_ref, store)


def inner_kernel(
    video_ref, w_ref, edge_ref, weight_ref, acc_ref, row_ref, middle_ref, tap_ref, row_sem, w_sem
):
    frames, rows, cols, channels = video_ref.shape
    w_copies = [
        pltpu.make_async_copy(w_ref.at[1, column], middle_ref.at[0, column], w_sem.at[column])
        for column in range(3)
    ]
    copies = {
        row: [
            pltpu.make_async_copy(
                video_ref.at[frame, whole_row(row, rows)],
                row_ref.at[row - 1, frame],
                row_sem.at[row - 1, frame],
            )
            for frame in range(frames)
        ]
        for row in range(1, rows - 1)
    }
    for copy in w_copies + [copy for group in copies.values() for copy in group]:
        copy.start()
    for copy in w_copies:
        copy.wait()

    def source_row(row):
        ref, at = (
            (edge_ref, 0) if row == 0 else (edge_ref, 1) if row == rows - 1 else (row_ref, row - 1)
        )
        return ref[at].reshape(frames * cols, channels)

    waited = set()
    for row in range(rows):
        total = None
        for step, (ref, at) in ((0, (middle_ref, 0)), (-1, (weight_ref, 1)), (1, (weight_ref, 0))):
            source = row + step
            if 0 <= source < rows:
                if source in copies and source not in waited:
                    waited.add(source)
                    for copy in copies[source]:
                        copy.wait()
                term = dot(source_row(source), tap_matrix(ref, at))
                total = term if total is None else total + term

        def store(frame, phase, value, row=row):
            acc_ref[row, frame, phase] = value

        place_phases(total, tap_ref, store)


def to_half(h, weight, frames, phases, count):
    return [
        dot(lanes([h(row, 2 * side + j) for row in range(2) for j in range(2)]), weight)
        .astype(BF16)
        .reshape(frames, count, -1)
        for side in range(phases // 2)
    ]


def near_kernel(acc_ref, near_ref, t_ref, r_ref, d_ref, h_out, h_ref):
    rows, frames, phases, count, channels = acc_ref.shape
    for row in range(1, rows):
        value = acc_ref[row]
        if row == rows - 1:
            value = value + near_ref[...].astype(F32)
        a = value.astype(BF16).reshape(frames, phases * count, channels)
        h_ref[row - 1] = silu(causal(a, t_ref)).astype(BF16).reshape(h_ref.shape[1:])
    h_out[...] = h_ref[0]
    weight = reduction(r_ref)
    for half in range(1, rows // 2):
        parts = to_half(
            lambda row, phase: h_ref[2 * half + row - 1, :, phase].reshape(
                frames * count, channels
            ),
            weight,
            frames,
            phases,
            count,
        )
        for side, part in enumerate(parts):
            d_ref[half - 1, :, side] = part


def far_kernel(acc_ref, far_ref, h_in, t_ref, r_ref, d_ref):
    _, frames, phases, count, channels = acc_ref.shape
    value = acc_ref[0] + inside(far_ref[...].astype(F32))
    a = value.astype(BF16).reshape(frames, phases * count, channels)
    h = silu(causal(a, t_ref)).astype(BF16).reshape(frames, phases, count, channels)
    parts = to_half(
        lambda row, phase: (h_in[:, phase] if row else h[:, phase]).reshape(
            frames * count, channels
        ),
        reduction(r_ref),
        frames,
        phases,
        count,
    )
    for side, part in enumerate(parts):
        d_ref[:, side] = part


def place_pairs(total, sites, count, channels):
    even, odd = total[:sites], total[sites:]
    first, middle, last = (slice(tap * channels, (tap + 1) * channels) for tap in range(3))
    return (
        shifted(odd[:, first], 1, count) + even[:, middle] + odd[:, last],
        even[:, first] + odd[:, middle] + shifted(even[:, last], -1, count),
    )


def flat(d):
    frames, sides, count, channels = d.shape
    return jnp.concatenate(
        [d[:, side].reshape(frames * count, channels) for side in range(sides)], axis=0
    )


def by_side(pair, shape):
    frames, _, count, channels = shape
    return jnp.stack([value.reshape(frames, count, channels) for value in pair], axis=1)


def second_rows(a, d, t_ref):
    frames, sides, count, channels = d.shape
    mixed = silu(causal(a.astype(BF16).reshape(frames, sides * count, channels), t_ref))
    return (d.astype(F32) + mixed.reshape(d.shape)).astype(BF16)


def middle_kernel(far_ref, rest_ref, near_ref, w_ref, t_ref, acc_ref, h_ref):
    shape = far_ref.shape
    frames, _, count, channels = shape
    sites = frames * count
    rows = rest_ref.shape[0] + 1
    side = turn()
    taps = {-1: 2 * side, 0: 1, 1: 2 - 2 * side}
    held = [far_ref[...]] + [rest_ref[row] for row in range(rows - 1)] + [near_ref[...]]
    for row in range(rows):
        total = None
        for step, tap in taps.items():
            if row + step >= 0:
                term = dot(flat(held[row + step]), tap_matrix(w_ref, tap))
                total = term if total is None else total + term
        a = by_side(place_pairs(total, sites, count, channels), shape)
        if row == 0:
            acc_ref[...] = a
        else:
            h_ref[row - 1] = second_rows(a, held[row], t_ref)


def second_kernel(
    acc_ref, far_ref, d_ref, rest_ref, w_ref, t_ref, r_ref, gain_ref, h_out, *blocks, group_size
):
    shape = d_ref.shape
    frames, _, count, channels = shape
    sites = frames * count
    more = dot(flat(inside(far_ref[...])), tap_matrix(w_ref, 2 * turn()))
    a = acc_ref[...] + by_side(place_pairs(more, sites, count, channels), shape)
    held = [second_rows(a, d_ref[...], t_ref)] + [rest_ref[row] for row in range(rest_ref.shape[0])]
    weight = reduction(r_ref)
    wide = weight.shape[-1]
    gain = gain_ref[...].astype(F32)
    place = lax.axis_index(AXIS) // group_size
    halves = len(held) // 2
    for half in range(halves):
        left = lanes(
            [held[2 * half + i][:, j].reshape(sites, channels) for i in range(2) for j in range(2)]
        )
        out_row = whole_row(half, halves) if halves > 1 else 0
        residual = dot(left, weight).astype(BF16)
        h_out[:, out_row] = residual.reshape(frames, count, wide)
        residual = residual.astype(F32)
        mean_square = jnp.mean(residual * residual, axis=-1, keepdims=True)
        normed = (residual * lax.rsqrt(mean_square + 1e-06) * gain).astype(BF16)
        normed = normed.reshape(frames, count, wide)
        for frame in range(frames):
            for step, block in enumerate(blocks):

                @pl.when(place ^ step == frame)
                def _(block=block, frame=frame, half=half, normed=normed):
                    at = out_row * count if halves > 1 else 0
                    block[pl.ds(at, count), :] = normed[frame]


def scored(mapped, sites):
    scores = lax.dot_general(
        mapped, sites, (((1,), (1,)), ((), ())), preferred_element_type=F32
    ) * (1.0 / math.sqrt(mapped.shape[-1]))
    top = jnp.max(scores, axis=-1, keepdims=True)
    weights = jnp.exp(scores - top)
    return top, jnp.sum(weights, axis=-1, keepdims=True), dot(weights.astype(BF16), sites)


def joined(left, right):
    top = jnp.maximum(left[0], right[0])
    one, two = jnp.exp(left[0] - top), jnp.exp(right[0] - top)
    return top, left[1] * one + right[1] * two, left[2] * one + right[2] * two


def query_kernel(own_ref, q_ref, k_ref, out_ref):
    queries = dot(own_ref[...], q_ref[...]).astype(BF16)
    out_ref[...] = lax.dot_general(
        queries, k_ref[...], (((1,), (1,)), ((), ())), preferred_element_type=F32
    ).astype(BF16)


def early_kernel(mapped_ref, *refs):
    *site_refs, top_ref, total_ref, mixed_ref = refs
    sites = jnp.concatenate([ref[...] for ref in site_refs], axis=0)
    top, total, mixed_ref[...] = scored(mapped_ref[...], sites)
    top_ref[...] = jnp.broadcast_to(top, top_ref.shape)
    total_ref[...] = jnp.broadcast_to(total, total_ref.shape)


def late_kernel(mapped_ref, top_ref, total_ref, mixed_ref, v_ref, o_ref, *refs, parts):
    site_refs, blocks = refs[:parts], refs[parts:]
    sites = jnp.concatenate([ref[...] for ref in site_refs], axis=0)
    early = top_ref[:, :1], total_ref[:, :1], mixed_ref[...]
    _, total, mixed = joined(early, scored(mapped_ref[...], sites))
    attended = dot((mixed / total).astype(BF16), v_ref[...]).astype(BF16)
    result = dot(attended, o_ref[...]).astype(BF16)
    count = blocks[0].shape[0]
    for step, block in enumerate(blocks):
        block[...] = result[step * count : (step + 1) * count]


def sum_kernel(h_ref, *refs, group_size):
    *blocks, out_ref = refs
    _, rows, count, channels = h_ref.shape
    place = lax.axis_index(AXIS) // group_size
    for step, block in enumerate(blocks):
        frame = place ^ step
        value = block[...].astype(F32).reshape(rows, count, channels)
        out_ref[frame] = (h_ref[frame].astype(F32) + value).astype(BF16)


def call(kernel, outs, scratch, args, flops, spaces=None, sems=(), limit=None):
    vmem = pl.BlockSpec(memory_space=pltpu.VMEM)
    shapes = [jax.ShapeDtypeStruct(shape, dtype) for shape, dtype in outs]
    moved = sum(math.prod(arg.shape) * arg.dtype.itemsize for arg in args)
    moved += sum(math.prod(shape) * jnp.dtype(dtype).itemsize for shape, dtype in outs)
    return pl.pallas_call(
        kernel,
        out_shape=shapes,
        in_specs=[pl.BlockSpec(memory_space=space) for space in spaces or [pltpu.VMEM] * len(args)],
        out_specs=[vmem] * len(outs),
        scratch_shapes=[pltpu.VMEM(shape, dtype) for shape, dtype in scratch] + list(sems),
        compiler_params=pltpu.CompilerParams(vmem_limit_bytes=limit or LIMIT),
        cost_estimate=pl.CostEstimate(flops=int(flops), bytes_accessed=int(moved), transcendentals=0),
    )(*args)


LIMIT = 40 * 1024 * 1024
WHOLE = 40 << 20


def per_device(
    video,
    s1_weight,
    t1_weight,
    r1_weight,
    s2_weight,
    t2_weight,
    r2_weight,
    attn_gain,
    w_query,
    w_key,
    w_value,
    w_out,
):
    frames, rows, cols, c0 = video.shape
    c1, c2, c3 = s1_weight.shape[-1], s2_weight.shape[-1], w_out.shape[-1]
    count = cols // PHASES
    devices = lax.axis_size(AXIS)
    group_size = devices // frames
    inner = [(d, d ^ 1) for d in range(devices)]
    groups = lax.axis_size("groups")
    outer = [(d, d + 1) for d in range(1, devices - 1, 2)]
    outer = outer + [(target, source) for source, target in outer]
    outer = [(g * devices + a, g * devices + b) for g in range(groups) for a, b in outer]
    if groups % 2 == 0:
        outer += [
            (g * devices + end, (g ^ 1) * devices + end)
            for g in range(groups)
            for end in (0, devices - 1)
        ]
    turns = [
        [(d, (d // group_size ^ k) * group_size + d % group_size) for d in range(devices)]
        for k in range(frames)
    ]

    edge = ((frames, PHASES, count, c1), BF16)
    taps = ((3, frames, cols, c1), F32)
    dma = pltpu.SemaphoreType.DMA
    site_flops = 2 * frames * cols * 3 * c0 * c1
    video = pltpu.with_memory_space_constraint(video, pltpu.HBM)
    s1_weight = pltpu.with_memory_space_constraint(s1_weight, pltpu.HBM)
    far, near, edge_rows, edge_weight = call(
        edge_kernel,
        [edge, edge, ((2, frames, cols, c0), BF16), ((2, 3, c0, c1), BF16)],
        [taps],
        [video, s1_weight],
        2 * site_flops,
        [pltpu.HBM] * 2,
        [dma((2, frames)), dma((2, 3))],
        WHOLE,
    )
    far = lax.ppermute(far, BOTH, outer)
    near = lax.ppermute(near, AXIS, inner)
    (acc,) = call(
        inner_kernel,
        [((rows, frames, PHASES, count, c1), F32)],
        [((rows - 2, frames, cols, c0), BF16), ((1, 3, c0, c1), BF16), taps],
        [video, s1_weight, edge_rows, edge_weight],
        10 * site_flops,
        [pltpu.HBM] * 2 + [pltpu.VMEM] * 2,
        [dma((rows - 2, frames)), dma((3,))],
        WHOLE,
    )
    half = (frames, 2, count, c2)
    rest = ((rows // 2 - 1, *half), BF16)
    rest_of, h_next = call(
        near_kernel,
        [rest, edge],
        [((rows - 1, frames, PHASES, count, c1), BF16)],
        [acc, near, t1_weight, r1_weight],
        4e8,
    )
    near = lax.ppermute(rest_of[-1], AXIS, inner)
    (d_far,) = call(far_kernel, [(half, BF16)], [], [acc, far, h_next, t1_weight, r1_weight], 2e8)
    far = lax.ppermute(d_far, BOTH, outer)
    acc, h_rest = call(
        middle_kernel, [(half, F32), rest], [], [d_far, rest_of, near, s2_weight, t2_weight], 9e8
    )
    site_rows = rows // 4
    block = ((site_rows * count, c3), BF16)
    residual, *blocks = call(
        functools.partial(second_kernel, group_size=group_size),
        [((frames, site_rows, count, c3), BF16)] + [block] * frames,
        [],
        [acc, far, d_far, h_rest, s2_weight, t2_weight, r2_weight, attn_gain.reshape(1, c3)],
        6e8,
    )
    own = jnp.concatenate(
        [blocks[0]] + [lax.ppermute(blocks[k], AXIS, turns[k]) for k in range(1, frames)], axis=0
    )
    site_count = own.shape[0]
    bits = []
    bit = group_size // 2
    while bit > 1:
        bits.append(bit)
        bit //= 2

    def swap(x, bit):
        return lax.ppermute(x, AXIS, [(d, d ^ bit) for d in range(devices)])

    far_sites = []
    have = [own]
    for bit in bits:
        whole = jnp.concatenate(have, axis=0) if len(have) > 1 else have[0]
        got = swap(whole, bit)
        far_sites.append(got)
        have = have + [got]
    (mapped,) = call(query_kernel, [(own.shape, BF16)], [], [own, w_query, w_key], 2e8)
    own, mapped = lax.optimization_barrier((own, mapped))
    partner = swap(own, 1)
    stats = ((site_count, 128), F32)
    early = call(early_kernel, [stats, stats, (own.shape, F32)], [], [mapped, own, partner], 3e8)
    far_sites = jnp.concatenate(far_sites, axis=0) if len(far_sites) > 1 else far_sites[0]
    far_sites, early = lax.optimization_barrier((far_sites, early))
    late = [far_sites, swap(far_sites, 1)]
    blocks = call(
        functools.partial(late_kernel, parts=len(late)),
        [block] * frames,
        [],
        [mapped, *early, w_value, w_out, *late],
        6e8,
    )
    blocks = [blocks[0]] + [lax.ppermute(blocks[k], AXIS, turns[k]) for k in range(1, frames)]
    (encoded,) = call(
        functools.partial(sum_kernel, group_size=group_size),
        [(residual.shape, BF16)],
        [],
        [residual, *blocks],
        1e6,
    )
    return encoded


def solution(mesh):
    placed = (P("groups", "ha", None, None), P(), P(), P(), P(), P(), P(), P(), P(), P(), P(), P())
    return jax.shard_map(
        per_device,
        mesh=mesh,
        in_specs=placed,
        out_specs=P("groups", "ha", None, None),
        check_vma=False,
    )
```

```python
import functools
import math

import jax
import jax.numpy as jnp
from jax import lax
from jax.experimental import pallas as pl
from jax.experimental.pallas import tpu as pltpu
from jax.sharding import PartitionSpec as P


F32 = jnp.float32
BF16 = jnp.bfloat16
AXIS = "ha"
BOTH = ("groups", AXIS)
PHASES = 4


Z_ORDER = (3, 1, 2)
Y_ORDER = (0, 3, 1, 2)


def dot(left, right):
    return jnp.dot(left, right, preferred_element_type=F32)


def turn():
    return lax.axis_index(AXIS) % 2


def whole_row(row, count):
    return row + turn() * (count - 1 - 2 * row)


def inside(far):
    index = lax.axis_index(AXIS)
    at_end = (index == 0) | (index == lax.axis_size(AXIS) - 1)
    return jnp.where(at_end, jnp.zeros_like(far), far)


def causal(a, t_ref, first=0):
    frames, sites, channels = a.shape
    total = None
    for lag in range(3):
        start = max(first - lag, 0)
        held = a[start : frames - lag]
        count = held.shape[0]
        if not count:
            continue
        term = dot(held.reshape(count * sites, channels), t_ref[2 - lag]).reshape(count, sites, -1)
        skip = frames - first - count
        if total is None:
            total = term
        elif skip:
            total = jnp.concatenate([total[:skip], total[skip:] + term], axis=0)
        else:
            total = total + term
    return total


def causal_pairs(a, t_ref, first=0):
    frames, _, channels = a.shape
    none = jnp.zeros_like(t_ref[0])
    results = []
    for frame in range(first, frames, 2):
        held = range(max(frame - 2, 0), frame + 2)

        def tap(source, target):
            lag = target - source
            return t_ref[2 - lag] if 0 <= lag <= 2 else none

        weight = jnp.concatenate(
            [lanes([tap(source, frame), tap(source, frame + 1)]) for source in held], axis=0
        )
        both = dot(lanes([a[source] for source in held]), weight)
        results += [both[:, :channels], both[:, channels:]]
    return jnp.stack(results, axis=0)


def reduction(r_ref):
    first = turn()
    return jnp.concatenate(
        [r_ref[first, 0], r_ref[first, 1], r_ref[1 - first, 0], r_ref[1 - first, 1]], axis=0
    )


def lanes(parts):
    return parts[0] if len(parts) == 1 else jnp.concatenate(parts, axis=-1)


def silu(x):
    return 0.5 * x * (1.0 + jnp.tanh(0.5 * x))


def shifted(x, step, period):
    rows, channels = x.shape
    place = lax.broadcasted_iota(jnp.int32, (rows // period, period, channels), 1)
    place = place.reshape(rows, channels)
    moved = pltpu.roll(x, step % rows, 0)
    return jnp.where(place == (0 if step == 1 else period - 1), 0.0, moved)


def place_phases(total, tap_ref, out_of):
    _, frames, cols, channels = tap_ref.shape
    count = cols // PHASES
    for tap in range(3):
        tap_ref[tap] = total[:, tap * channels : (tap + 1) * channels].reshape(
            frames, cols, channels
        )
    for frame in range(frames):
        def strided(tap, phase):
            return tap_ref[tap, frame, pl.ds(phase, count, stride=PHASES), :]

        for phase in range(PHASES):
            before = (
                shifted(strided(0, PHASES - 1), 1, count)
                if phase == 0
                else strided(0, phase - 1)
            )
            after = (
                shifted(strided(2, 0), -1, count)
                if phase == PHASES - 1
                else strided(2, phase + 1)
            )
            out_of(frame, phase, before + strided(1, phase) + after)


def tap_matrix(w_ref, row):
    return lanes([w_ref[row, tap] for tap in range(3)])


def fetch_rows(video_ref, row, first, rows_to, sem):
    copies = [
        pltpu.make_async_copy(video_ref.at[first + at, row], rows_to.at[at], sem.at[at])
        for at in range(rows_to.shape[0])
    ]
    for copy in copies:
        copy.start()
    return copies


def fetch_taps(w_ref, tap, taps_to, sem):
    copies = [
        pltpu.make_async_copy(w_ref.at[tap, column], taps_to.at[column], sem.at[column])
        for column in range(taps_to.shape[0])
    ]
    for copy in copies:
        copy.start()
    return copies


def finish(copies):
    for copy in copies:
        copy.wait()


def edge_of(rows, taps_ref, tap_ref, out_ref):
    frames, cols, channels = rows.shape
    weight = lanes([taps_ref[column] for column in range(3)])
    total = dot(rows.reshape(frames * cols, channels), weight)

    def store(frame, phase, value):
        out_ref[frame, phase] = value.astype(BF16)

    place_phases(total, tap_ref.at[:, :frames], store)


def first_edge_kernel(video_ref, w_ref, out_ref, rows_to, taps_to, tap_ref, row_sem, tap_sem):
    side = turn()
    row = whole_row(0, video_ref.shape[1])
    copies = fetch_taps(w_ref, 2 - 2 * side, taps_to, tap_sem)
    finish(fetch_rows(video_ref, row, 0, rows_to, row_sem) + copies)
    edge_of(rows_to[...], taps_to, tap_ref, out_ref)


def rest_edge_kernel(video_ref, w_ref, far_out, near_out, tap_ref):
    frames, rows = video_ref.shape[:2]
    side = turn()
    first = frames - far_out.shape[0]
    far = video_ref[first:, whole_row(0, rows)]
    edge_of(far, w_ref.at[2 - 2 * side], tap_ref, far_out)
    edge_of(video_ref[:, whole_row(rows - 1, rows)], w_ref.at[2 * side], tap_ref, near_out)


def inner_rows(wanted, video_ref, w_ref, tap_ref, store_of):
    frames, rows, cols, channels = video_ref.shape
    side = turn()
    taps = {0: 1, -1: 2 * side, 1: 2 - 2 * side}
    totals = {}
    for source in range(max(wanted[0] - 1, 0), min(wanted[-1] + 2, rows)):
        steps = [step for step in taps if source - step in wanted]
        weight = lanes([tap_matrix(w_ref, taps[step]) for step in steps])
        held = video_ref[:, whole_row(source, rows)].reshape(frames * cols, channels)
        terms = dot(held, weight)
        wide = terms.shape[-1] // len(steps)
        for at, step in enumerate(steps):
            term = terms[:, at * wide : (at + 1) * wide]
            row = source - step
            totals[row] = totals[row] + term if row in totals else term
    for row in wanted:
        place_phases(totals[row], tap_ref, store_of(row))


def front_kernel(video_ref, w_ref, t_ref, acc_ref, h_ref, one_ref, tap_ref):
    frames, phases, count, channels = acc_ref.shape

    def store_of(row):
        def store(frame, phase, value):
            if row == 0:
                acc_ref[frame, phase] = value
            else:
                one_ref[frame, phase] = value.astype(BF16)

        return store

    inner_rows((0, 1), video_ref, w_ref, tap_ref, store_of)
    a = one_ref[...].reshape(frames, phases * count, channels)
    h_ref[...] = silu(causal_pairs(a, t_ref)).astype(BF16).reshape(h_ref.shape)


def to_half(h, weight, frames, phases, count):
    return [
        dot(lanes([h(row, 2 * side + j) for row in range(2) for j in range(2)]), weight)
        .astype(BF16)
        .reshape(frames, count, -1)
        for side in range(phases // 2)
    ]


def far_kernel(acc_ref, far_ref, h_in, t_ref, r_ref, *refs, first):
    frames, phases, count, channels = far_ref.shape
    mine = pl.ds(first, frames)
    a = (acc_ref[mine] + inside(far_ref[...].astype(F32))).astype(BF16)
    if first:
        before_ref, d_ref = refs
        whole = jnp.concatenate([before_ref[...], a], axis=0)
    else:
        d_ref, a_ref = refs
        a_ref[...] = a
        whole = a
    whole = whole.reshape(whole.shape[0], phases * count, channels)
    h = silu(causal(whole, t_ref, first)).astype(BF16).reshape(frames, phases, count, channels)
    parts = to_half(
        lambda row, phase: (h_in[mine, phase] if row else h[:, phase]).reshape(
            frames * count, channels
        ),
        reduction(r_ref),
        frames,
        phases,
        count,
    )
    for side, part in enumerate(parts):
        d_ref[:, side] = part


def back_rows_kernel(
    video_ref, w_ref, near_ref, t_ref, r_ref, d_ref, acc_ref, h_ref, tap_ref
):
    frames, phases, count, channels = near_ref.shape
    last = video_ref.shape[1] - 1

    def store_of(row):
        def store(frame, phase, value):
            if row == last:
                value = value + near_ref[frame, phase].astype(F32)
            acc_ref[row - 2, frame, phase] = value.astype(BF16)

        return store

    inner_rows(range(2, last + 1), video_ref, w_ref, tap_ref, store_of)
    for row in range(2, last + 1):
        a = acc_ref[row - 2].reshape(frames, phases * count, channels)
        h_ref[row - 2] = silu(causal(a, t_ref)).astype(BF16).reshape(h_ref.shape[1:])
    weight = reduction(r_ref)
    for half in range(d_ref.shape[0]):
        parts = to_half(
            lambda row, phase: h_ref[2 * half + row, :, phase].reshape(frames * count, channels),
            weight,
            frames,
            phases,
            count,
        )
        for side, part in enumerate(parts):
            d_ref[half, :, side] = part


def place_pairs(total, sites, count, channels):
    even, odd = total[:sites], total[sites:]
    first, middle, last = (slice(tap * channels, (tap + 1) * channels) for tap in range(3))
    return (
        shifted(odd[:, first], 1, count) + even[:, middle] + odd[:, last],
        even[:, first] + odd[:, middle] + shifted(even[:, last], -1, count),
    )


def flat(d):
    frames, sides, count, channels = d.shape
    return jnp.concatenate(
        [d[:, side].reshape(frames * count, channels) for side in range(sides)], axis=0
    )


def by_side(pair, shape):
    frames, _, count, channels = shape
    return jnp.stack([value.reshape(frames, count, channels) for value in pair], axis=1)


def second_rows(a, d, t_ref, first=0):
    _, sides, count, channels = d.shape
    mixed = silu(causal(a.reshape(a.shape[0], sides * count, channels), t_ref, first))
    return (d.astype(F32) + mixed.reshape(d.shape)).astype(BF16)


def middle_kernel(far_a_ref, far_b_ref, rest_ref, near_ref, w_ref, t_ref, acc_ref, h_ref):
    shape = near_ref.shape
    frames, _, count, channels = shape
    sites = frames * count
    rows = rest_ref.shape[0] + 1
    side = turn()
    taps = {-1: 2 * side, 0: 1, 1: 2 - 2 * side}
    held = [jnp.concatenate([far_a_ref[...], far_b_ref[...]], axis=0)]
    held += [rest_ref[row] for row in range(rows - 1)] + [near_ref[...]]
    for row in range(rows):
        total = None
        for step, tap in taps.items():
            if row + step >= 0:
                term = dot(flat(held[row + step]), tap_matrix(w_ref, tap))
                total = term if total is None else total + term
        a = by_side(place_pairs(total, sites, count, channels), shape)
        if row == 0:
            acc_ref[...] = a
        else:
            h_ref[row - 1] = second_rows(a.astype(BF16), held[row], t_ref)


def second_kernel(
    acc_ref, far_ref, d_ref, rest_ref, w_ref, t_ref, r_ref, gain_ref, *refs, first, group_size
):
    shape = d_ref.shape
    frames, _, count, channels = shape
    sites = frames * count
    mine = pl.ds(first, frames)
    more = dot(flat(inside(far_ref[...])), tap_matrix(w_ref, 2 * turn()))
    a = acc_ref[mine] + by_side(place_pairs(more, sites, count, channels), shape)
    a = a.astype(BF16)
    if first:
        before_ref, done_ref, h_out, *blocks = refs
        whole = jnp.concatenate([before_ref[...], a], axis=0)
    else:
        h_out, a_out, normed_out = refs
        a_out[...] = a
        whole = a
    held = [second_rows(whole, d_ref[...], t_ref, first)]
    held += [rest_ref[row, mine] for row in range(rest_ref.shape[0])]
    weight = reduction(r_ref)
    wide = weight.shape[-1]
    gain = gain_ref[...].astype(F32)
    place = lax.axis_index(AXIS) // group_size
    halves = len(held) // 2
    for half in range(halves):
        left = lanes(
            [held[2 * half + i][:, j].reshape(sites, channels) for i in range(2) for j in range(2)]
        )
        out_row = whole_row(half, halves) if halves > 1 else 0
        residual = dot(left, weight).astype(BF16)
        h_out[:, out_row] = residual.reshape(frames, count, wide)
        residual = residual.astype(F32)
        mean_square = jnp.mean(residual * residual, axis=-1, keepdims=True)
        normed = (residual * lax.rsqrt(mean_square + 1e-06) * gain).astype(BF16)
        normed = normed.reshape(frames, count, wide)
        if not first:
            normed_out[:, out_row] = normed
            continue
        ready = [done_ref[frame, out_row] for frame in range(first)]
        ready += [normed[frame] for frame in range(frames)]
        for frame, value in enumerate(ready):
            for step, block in enumerate(blocks):

                @pl.when(place ^ step == frame)
                def _(block=block, value=value, out_row=out_row):
                    at = out_row * count if halves > 1 else 0
                    block[pl.ds(at, count), :] = value


def scored(mapped, sites):
    scores = lax.dot_general(
        mapped, sites, (((1,), (1,)), ((), ())), preferred_element_type=F32
    ) * (1.0 / math.sqrt(mapped.shape[-1]))
    top = jnp.max(scores, axis=-1, keepdims=True)
    weights = jnp.exp(scores - top)
    return top, jnp.sum(weights, axis=-1, keepdims=True), dot(weights.astype(BF16), sites)


def joined(left, right):
    top = jnp.maximum(left[0], right[0])
    one, two = jnp.exp(left[0] - top), jnp.exp(right[0] - top)
    return top, left[1] * one + right[1] * two, left[2] * one + right[2] * two


def maps_kernel(q_ref, k_ref, v_ref, o_ref, score_ref, out_ref):
    score_ref[...] = lax.dot_general(
        q_ref[...], k_ref[...], (((1,), (1,)), ((), ())), preferred_element_type=F32
    ).astype(BF16)
    out_ref[...] = dot(v_ref[...], o_ref[...]).astype(BF16)


def query_kernel(own_ref, map_ref, out_ref):
    out_ref[...] = dot(own_ref[...], map_ref[...]).astype(BF16)


def early_kernel(mapped_ref, *refs):
    site_refs, outs = refs[:-3], refs[-3:]
    keep(scored(mapped_ref[...], sites_of(site_refs)), *outs)


def keep(stats, top_ref, total_ref, mixed_ref):
    top, total, mixed_ref[...] = stats
    top_ref[...] = jnp.broadcast_to(top, top_ref.shape)
    total_ref[...] = jnp.broadcast_to(total, total_ref.shape)


def sites_of(refs):
    return refs[0][...] if len(refs) == 1 else jnp.concatenate([ref[...] for ref in refs], axis=0)


def next_kernel(mapped_ref, top_ref, total_ref, mixed_ref, *refs):
    site_refs, outs = refs[:-3], refs[-3:]
    held = top_ref[:, :1], total_ref[:, :1], mixed_ref[...]
    keep(joined(held, scored(mapped_ref[...], sites_of(site_refs))), *outs)


def late_kernel(mapped_ref, top_ref, total_ref, mixed_ref, map_ref, *refs, first, parts):
    site_refs, blocks = refs[:parts], refs[parts:]
    count = blocks[0].shape[0]
    mine = slice(first * count, (first + len(blocks)) * count)
    held = top_ref[mine, :1], total_ref[mine, :1], mixed_ref[mine]
    _, total, mixed = joined(held, scored(mapped_ref[mine], sites_of(site_refs)))
    result = dot((mixed / total).astype(BF16), map_ref[...]).astype(BF16)
    for step, block in enumerate(blocks):
        block[...] = result[step * count : (step + 1) * count]


def sum_kernel(a_ref, b_ref, *refs, group_size):
    *blocks, out_ref = refs
    first, rows, count, channels = a_ref.shape
    place = lax.axis_index(AXIS) // group_size
    for step, block in enumerate(blocks):
        value = block[...].astype(F32).reshape(rows, count, channels)
        frame = place ^ step

        @pl.when(frame < first)
        def _(value=value, frame=frame):
            out_ref[frame] = (a_ref[frame].astype(F32) + value).astype(BF16)

        @pl.when(frame >= first)
        def _(value=value, frame=frame):
            out_ref[frame] = (b_ref[frame - first].astype(F32) + value).astype(BF16)


def call(kernel, outs, scratch, args, flops, spaces=None, sems=(), limit=None):
    vmem = pl.BlockSpec(memory_space=pltpu.VMEM)
    shapes = [jax.ShapeDtypeStruct(shape, dtype) for shape, dtype in outs]
    moved = sum(math.prod(arg.shape) * arg.dtype.itemsize for arg in args)
    moved += sum(math.prod(shape) * jnp.dtype(dtype).itemsize for shape, dtype in outs)
    return pl.pallas_call(
        kernel,
        out_shape=shapes,
        in_specs=[pl.BlockSpec(memory_space=space) for space in spaces or [pltpu.VMEM] * len(args)],
        out_specs=[vmem] * len(outs),
        scratch_shapes=[pltpu.VMEM(shape, dtype) for shape, dtype in scratch] + list(sems),
        compiler_params=pltpu.CompilerParams(vmem_limit_bytes=limit or LIMIT),
        cost_estimate=pl.CostEstimate(flops=int(flops), bytes_accessed=int(moved), transcendentals=0),
    )(*args)


LIMIT = 40 * 1024 * 1024


def per_device(
    video,
    s1_weight,
    t1_weight,
    r1_weight,
    s2_weight,
    t2_weight,
    r2_weight,
    attn_gain,
    w_query,
    w_key,
    w_value,
    w_out,
):
    frames, rows, cols, c0 = video.shape
    c1, c2, c3 = s1_weight.shape[-1], s2_weight.shape[-1], w_out.shape[-1]
    count = cols // PHASES
    devices = lax.axis_size(AXIS)
    group_size = devices // frames
    inner = [(d, d ^ 1) for d in range(devices)]
    groups = lax.axis_size("groups")
    outer = [(d, d + 1) for d in range(1, devices - 1, 2)]
    outer = outer + [(target, source) for source, target in outer]
    outer = [(g * devices + a, g * devices + b) for g in range(groups) for a, b in outer]
    if groups % 2 == 0:
        outer += [
            (g * devices + end, (g ^ 1) * devices + end)
            for g in range(groups)
            for end in (0, devices - 1)
        ]
    turns = [
        [(d, (d // group_size ^ k) * group_size + d % group_size) for d in range(devices)]
        for k in range(frames)
    ]

    edge = ((frames, PHASES, count, c1), BF16)
    taps = ((3, frames, cols, c1), F32)
    dma = pltpu.SemaphoreType.DMA
    site_flops = 2 * frames * cols * 3 * c0 * c1
    held = [pltpu.with_memory_space_constraint(x, pltpu.VMEM) for x in (video, s1_weight)]
    video = pltpu.with_memory_space_constraint(video, pltpu.HBM)
    s1_weight = pltpu.with_memory_space_constraint(s1_weight, pltpu.HBM)
    hbm = pltpu.HBM
    part = frames // 2

    (far_a,) = call(
        first_edge_kernel,
        [((part, *edge[0][1:]), BF16)],
        [((part, cols, c0), BF16), ((3, c0, c1), BF16), taps],
        [video, s1_weight],
        site_flops // 2,
        [hbm] * 2,
        [dma((part,)), dma((3,))],
    )
    far_a = lax.ppermute(far_a, BOTH, outer)
    later = frames - part
    far_b, near = call(
        rest_edge_kernel, [((later, *edge[0][1:]), BF16), edge], [taps], held, site_flops * 1.5
    )
    far_b = lax.ppermute(far_b, BOTH, outer)
    near = lax.ppermute(near, AXIS, inner)
    acc, h_next = call(
        front_kernel, [(edge[0], F32), edge], [edge, taps], [*held, t1_weight], 5 * site_flops
    )
    half = (frames, 2, count, c2)
    d_a, a_one = call(
        functools.partial(far_kernel, first=0),
        [((part, *half[1:]), BF16), ((part, *edge[0][1:]), BF16)],
        [],
        [acc, far_a, h_next, t1_weight, r1_weight],
        1e8,
    )
    far_two = lax.ppermute(d_a, BOTH, outer)
    rest = ((rows // 2 - 1, *half), BF16)
    left_rows = ((rows - 2, *edge[0]), BF16)
    (rest_of,) = call(
        back_rows_kernel,
        [rest],
        [left_rows, left_rows, taps],
        [*held, near, t1_weight, r1_weight],
        9e8,
    )
    near = lax.ppermute(rest_of[-1], AXIS, inner)
    (d_b,) = call(
        functools.partial(far_kernel, first=part),
        [((later, *half[1:]), BF16)],
        [],
        [acc, far_b, h_next, t1_weight, r1_weight, a_one],
        1e8,
    )
    far_two_b = lax.ppermute(d_b, BOTH, outer)
    acc, h_rest = call(
        middle_kernel, [(half, F32), rest], [], [d_a, d_b, rest_of, near, s2_weight, t2_weight], 9e8
    )
    site_rows = rows // 4
    block = ((site_rows * count, c3), BF16)
    gain = attn_gain.reshape(1, c3)
    site = ((part, site_rows, count, c3), BF16)
    residual_a, a_two, normed = call(
        functools.partial(second_kernel, first=0, group_size=group_size),
        [site, ((part, *half[1:]), BF16), site],
        [],
        [acc, far_two, d_a, h_rest, s2_weight, t2_weight, r2_weight, gain],
        3e8,
    )
    residual_b, *blocks = call(
        functools.partial(second_kernel, first=part, group_size=group_size),
        [((later, *site[0][1:]), BF16)] + [block] * frames,
        [],
        [acc, far_two_b, d_b, h_rest, s2_weight, t2_weight, r2_weight, gain, a_two, normed],
        3e8,
    )

    def swap(x, bit):
        return lax.ppermute(x, AXIS, [(d, d ^ bit) for d in range(devices)])

    def join(parts):
        return parts[0] if len(parts) == 1 else jnp.concatenate(parts, axis=0)

    held_blocks = [blocks[0]] + [lax.ppermute(blocks[k], AXIS, turns[k]) for k in range(1, frames)]
    order = (0, *Z_ORDER)
    own = join([held_blocks[k] for k in order])
    bit = group_size // 2
    first_far = [swap(held_blocks[k], bit) for k in Y_ORDER]
    if bit == 2:
        near_parts, last_parts = first_far[:-1], [first_far[-1]]
        last_parts.append(swap(held_blocks[Y_ORDER[-1]], bit + 1))
    else:
        near_parts, last_parts = [join(first_far)], []
        bit //= 2
        while bit > 1:
            near_parts.append(swap(join([own] + near_parts), bit))
            bit //= 2
    weight = ((c3, c3), BF16)
    score_map, out_map = call(
        maps_kernel, [weight, weight], [], [w_query, w_key, w_value, w_out], 5e8
    )
    partner = swap(own, 1)
    (mapped,) = call(query_kernel, [(own.shape, BF16)], [], [own, score_map], 1e8)
    stats = ((own.shape[0], 128), F32)
    sums = [stats, stats, (own.shape, F32)]
    early = call(early_kernel, sums, [], [mapped, own, partner], 3e8)
    near_parts, early = lax.optimization_barrier((near_parts, early))
    far_sites = join(near_parts)
    last_parts.append(swap(far_sites, 1))
    held_sums = call(next_kernel, sums, [], [mapped, *early, far_sites], 2e8)

    def late_blocks(first, after):
        return call(
            functools.partial(late_kernel, first=first, parts=len(last_parts)),
            [block] * (after - first),
            [],
            [mapped, *held_sums, out_map, *last_parts],
            3e8,
        )

    done = dict(zip(order, late_blocks(0, frames)))
    blocks = [done[0]] + [lax.ppermute(done[k], AXIS, turns[k]) for k in range(1, frames)]
    (encoded,) = call(
        functools.partial(sum_kernel, group_size=group_size),
        [((frames, site_rows, count, c3), BF16)],
        [],
        [residual_a, residual_b, *blocks],
        1e6,
    )
    return encoded


def solution(mesh):
    placed = (P("groups", "ha", None, None), P(), P(), P(), P(), P(), P(), P(), P(), P(), P(), P())
    return jax.shard_map(
        per_device,
        mesh=mesh,
        in_specs=placed,
        out_specs=P("groups", "ha", None, None),
        check_vma=False,
    )
```

```python
import functools
import math

import jax
import jax.numpy as jnp
from jax import lax
from jax.experimental import pallas as pl
from jax.experimental.pallas import tpu as pltpu
from jax.sharding import PartitionSpec as P


F32 = jnp.float32
BF16 = jnp.bfloat16
AXIS = "ha"
BOTH = ("groups", AXIS)
PHASES = 4


def dot(left, right):
    return jnp.dot(left, right, preferred_element_type=F32)


def turn():
    return lax.axis_index(AXIS) % 2


def whole_row(row, count):
    return row + turn() * (count - 1 - 2 * row)


def inside(far):
    index = lax.axis_index(AXIS)
    at_end = (index == 0) | (index == lax.axis_size(AXIS) - 1)
    return jnp.where(at_end, jnp.zeros_like(far), far)


def causal(a, t_ref, first=0):
    frames, sites, channels = a.shape
    total = None
    for lag in range(3):
        start = max(first - lag, 0)
        held = a[start : frames - lag]
        count = held.shape[0]
        if not count:
            continue
        term = dot(held.reshape(count * sites, channels), t_ref[2 - lag]).reshape(count, sites, -1)
        skip = frames - first - count
        if total is None:
            total = term
        elif skip:
            total = jnp.concatenate([total[:skip], total[skip:] + term], axis=0)
        else:
            total = total + term
    return total


def causal_pairs(a, t_ref, first=0):
    frames, _, channels = a.shape
    none = jnp.zeros_like(t_ref[0])
    results = []
    for frame in range(first, frames, 2):
        held = range(max(frame - 2, 0), frame + 2)

        def tap(source, target):
            lag = target - source
            return t_ref[2 - lag] if 0 <= lag <= 2 else none

        weight = jnp.concatenate(
            [lanes([tap(source, frame), tap(source, frame + 1)]) for source in held], axis=0
        )
        both = dot(lanes([a[source] for source in held]), weight)
        results += [both[:, :channels], both[:, channels:]]
    return jnp.stack(results, axis=0)


def reduction(r_ref):
    first = turn()
    return jnp.concatenate(
        [r_ref[first, 0], r_ref[first, 1], r_ref[1 - first, 0], r_ref[1 - first, 1]], axis=0
    )


def lanes(parts):
    return parts[0] if len(parts) == 1 else jnp.concatenate(parts, axis=-1)


def silu(x):
    return 0.5 * x * (1.0 + jnp.tanh(0.5 * x))


def shifted(x, step, period):
    rows, channels = x.shape
    place = lax.broadcasted_iota(jnp.int32, (rows // period, period, channels), 1)
    place = place.reshape(rows, channels)
    moved = pltpu.roll(x, step % rows, 0)
    return jnp.where(place == (0 if step == 1 else period - 1), 0.0, moved)


def place_phases(total, tap_ref, out_of):
    _, frames, cols, channels = tap_ref.shape
    count = cols // PHASES
    for tap in range(3):
        tap_ref[tap] = total[:, tap * channels : (tap + 1) * channels].reshape(
            frames, cols, channels
        )
    for frame in range(frames):
        def strided(tap, phase):
            return tap_ref[tap, frame, pl.ds(phase, count, stride=PHASES), :]

        for phase in range(PHASES):
            before = (
                shifted(strided(0, PHASES - 1), 1, count)
                if phase == 0
                else strided(0, phase - 1)
            )
            after = (
                shifted(strided(2, 0), -1, count)
                if phase == PHASES - 1
                else strided(2, phase + 1)
            )
            out_of(frame, phase, before + strided(1, phase) + after)


def tap_matrix(w_ref, row):
    return lanes([w_ref[row, tap] for tap in range(3)])


def fetch_rows(video_ref, row, first, rows_to, sem):
    copies = [
        pltpu.make_async_copy(video_ref.at[first + at, row], rows_to.at[at], sem.at[at])
        for at in range(rows_to.shape[0])
    ]
    for copy in copies:
        copy.start()
    return copies


def fetch_taps(w_ref, tap, taps_to, sem):
    copies = [
        pltpu.make_async_copy(w_ref.at[tap, column], taps_to.at[column], sem.at[column])
        for column in range(taps_to.shape[0])
    ]
    for copy in copies:
        copy.start()
    return copies


def finish(copies):
    for copy in copies:
        copy.wait()


def edge_of(rows, taps_ref, tap_ref, out_ref):
    frames, cols, channels = rows.shape
    weight = lanes([taps_ref[column] for column in range(3)])
    total = dot(rows.reshape(frames * cols, channels), weight)

    def store(frame, phase, value):
        out_ref[frame, phase] = value.astype(BF16)

    place_phases(total, tap_ref.at[:, :frames], store)


def first_edge_kernel(video_ref, w_ref, out_ref, rows_to, taps_to, tap_ref, row_sem, tap_sem):
    side = turn()
    row = whole_row(0, video_ref.shape[1])
    copies = fetch_taps(w_ref, 2 - 2 * side, taps_to, tap_sem)
    finish(fetch_rows(video_ref, row, 0, rows_to, row_sem) + copies)
    edge_of(rows_to[...], taps_to, tap_ref, out_ref)


def rest_edge_kernel(video_ref, w_ref, far_out, near_out, tap_ref):
    frames, rows = video_ref.shape[:2]
    side = turn()
    first = frames - far_out.shape[0]
    far = video_ref[first:, whole_row(0, rows)]
    edge_of(far, w_ref.at[2 - 2 * side], tap_ref, far_out)
    edge_of(video_ref[:, whole_row(rows - 1, rows)], w_ref.at[2 * side], tap_ref, near_out)


def inner_rows(wanted, video_ref, w_ref, tap_ref, store_of):
    frames, rows, cols, channels = video_ref.shape
    side = turn()
    taps = {0: 1, -1: 2 * side, 1: 2 - 2 * side}
    totals = {}
    for source in range(max(wanted[0] - 1, 0), min(wanted[-1] + 2, rows)):
        steps = [step for step in taps if source - step in wanted]
        weight = lanes([tap_matrix(w_ref, taps[step]) for step in steps])
        held = video_ref[:, whole_row(source, rows)].reshape(frames * cols, channels)
        terms = dot(held, weight)
        wide = terms.shape[-1] // len(steps)
        for at, step in enumerate(steps):
            term = terms[:, at * wide : (at + 1) * wide]
            row = source - step
            totals[row] = totals[row] + term if row in totals else term
    for row in wanted:
        place_phases(totals[row], tap_ref, store_of(row))


def front_kernel(video_ref, w_ref, t_ref, acc_ref, h_ref, one_ref, tap_ref):
    frames, phases, count, channels = acc_ref.shape

    def store_of(row):
        def store(frame, phase, value):
            if row == 0:
                acc_ref[frame, phase] = value
            else:
                one_ref[frame, phase] = value.astype(BF16)

        return store

    inner_rows((0, 1), video_ref, w_ref, tap_ref, store_of)
    a = one_ref[...].reshape(frames, phases * count, channels)
    h_ref[...] = silu(causal_pairs(a, t_ref)).astype(BF16).reshape(h_ref.shape)


def to_half(h, weight, frames, phases, count):
    return [
        dot(lanes([h(row, 2 * side + j) for row in range(2) for j in range(2)]), weight)
        .astype(BF16)
        .reshape(frames, count, -1)
        for side in range(phases // 2)
    ]


def far_kernel(acc_ref, far_ref, h_in, t_ref, r_ref, *refs, first):
    frames, phases, count, channels = far_ref.shape
    mine = pl.ds(first, frames)
    a = (acc_ref[mine] + inside(far_ref[...].astype(F32))).astype(BF16)
    if first:
        before_ref, d_ref = refs
        whole = jnp.concatenate([before_ref[...], a], axis=0)
    else:
        d_ref, a_ref = refs
        a_ref[...] = a
        whole = a
    whole = whole.reshape(whole.shape[0], phases * count, channels)
    h = silu(causal(whole, t_ref, first)).astype(BF16).reshape(frames, phases, count, channels)
    parts = to_half(
        lambda row, phase: (h_in[mine, phase] if row else h[:, phase]).reshape(
            frames * count, channels
        ),
        reduction(r_ref),
        frames,
        phases,
        count,
    )
    for side, part in enumerate(parts):
        d_ref[:, side] = part


def back_rows_kernel(
    video_ref, w_ref, near_ref, t_ref, r_ref, d_ref, acc_ref, h_ref, tap_ref
):
    frames, phases, count, channels = near_ref.shape
    last = video_ref.shape[1] - 1

    def store_of(row):
        def store(frame, phase, value):
            if row == last:
                value = value + near_ref[frame, phase].astype(F32)
            acc_ref[row - 2, frame, phase] = value.astype(BF16)

        return store

    inner_rows(range(2, last + 1), video_ref, w_ref, tap_ref, store_of)
    for row in range(2, last + 1):
        a = acc_ref[row - 2].reshape(frames, phases * count, channels)
        h_ref[row - 2] = silu(causal(a, t_ref)).astype(BF16).reshape(h_ref.shape[1:])
    weight = reduction(r_ref)
    for half in range(d_ref.shape[0]):
        parts = to_half(
            lambda row, phase: h_ref[2 * half + row, :, phase].reshape(frames * count, channels),
            weight,
            frames,
            phases,
            count,
        )
        for side, part in enumerate(parts):
            d_ref[half, :, side] = part


def place_pairs(total, sites, count, channels):
    even, odd = total[:sites], total[sites:]
    first, middle, last = (slice(tap * channels, (tap + 1) * channels) for tap in range(3))
    return (
        shifted(odd[:, first], 1, count) + even[:, middle] + odd[:, last],
        even[:, first] + odd[:, middle] + shifted(even[:, last], -1, count),
    )


def flat(d):
    frames, sides, count, channels = d.shape
    return jnp.concatenate(
        [d[:, side].reshape(frames * count, channels) for side in range(sides)], axis=0
    )


def by_side(pair, shape):
    frames, _, count, channels = shape
    return jnp.stack([value.reshape(frames, count, channels) for value in pair], axis=1)


def second_rows(a, d, t_ref, first=0):
    _, sides, count, channels = d.shape
    mixed = silu(causal(a.reshape(a.shape[0], sides * count, channels), t_ref, first))
    return (d.astype(F32) + mixed.reshape(d.shape)).astype(BF16)


def middle_kernel(far_a_ref, far_b_ref, rest_ref, near_ref, w_ref, t_ref, acc_ref, h_ref):
    shape = near_ref.shape
    frames, _, count, channels = shape
    sites = frames * count
    rows = rest_ref.shape[0] + 1
    side = turn()
    taps = {-1: 2 * side, 0: 1, 1: 2 - 2 * side}
    held = [jnp.concatenate([far_a_ref[...], far_b_ref[...]], axis=0)]
    held += [rest_ref[row] for row in range(rows - 1)] + [near_ref[...]]
    for row in range(rows):
        total = None
        for step, tap in taps.items():
            if row + step >= 0:
                term = dot(flat(held[row + step]), tap_matrix(w_ref, tap))
                total = term if total is None else total + term
        a = by_side(place_pairs(total, sites, count, channels), shape)
        if row == 0:
            acc_ref[...] = a
        else:
            h_ref[row - 1] = second_rows(a.astype(BF16), held[row], t_ref)


def second_kernel(
    acc_ref, far_ref, d_ref, rest_ref, w_ref, t_ref, r_ref, gain_ref, *refs, first, group_size
):
    shape = d_ref.shape
    frames, _, count, channels = shape
    sites = frames * count
    mine = pl.ds(first, frames)
    more = dot(flat(inside(far_ref[...])), tap_matrix(w_ref, 2 * turn()))
    a = acc_ref[mine] + by_side(place_pairs(more, sites, count, channels), shape)
    a = a.astype(BF16)
    if first:
        before_ref, done_ref, h_out, *blocks = refs
        whole = jnp.concatenate([before_ref[...], a], axis=0)
    else:
        h_out, a_out, normed_out = refs
        a_out[...] = a
        whole = a
    held = [second_rows(whole, d_ref[...], t_ref, first)]
    held += [rest_ref[row, mine] for row in range(rest_ref.shape[0])]
    weight = reduction(r_ref)
    wide = weight.shape[-1]
    gain = gain_ref[...].astype(F32)
    place = lax.axis_index(AXIS) // group_size
    halves = len(held) // 2
    for half in range(halves):
        left = lanes(
            [held[2 * half + i][:, j].reshape(sites, channels) for i in range(2) for j in range(2)]
        )
        out_row = whole_row(half, halves) if halves > 1 else 0
        residual = dot(left, weight).astype(BF16)
        h_out[:, out_row] = residual.reshape(frames, count, wide)
        residual = residual.astype(F32)
        mean_square = jnp.mean(residual * residual, axis=-1, keepdims=True)
        normed = (residual * lax.rsqrt(mean_square + 1e-06) * gain).astype(BF16)
        normed = normed.reshape(frames, count, wide)
        if not first:
            normed_out[:, out_row] = normed
            continue
        ready = [done_ref[frame, out_row] for frame in range(first)]
        ready += [normed[frame] for frame in range(frames)]
        for frame, value in enumerate(ready):
            for step, block in enumerate(blocks):

                @pl.when(place ^ step == frame)
                def _(block=block, value=value, out_row=out_row):
                    at = out_row * count if halves > 1 else 0
                    block[pl.ds(at, count), :] = value


def scored(mapped, sites):
    scores = lax.dot_general(
        mapped, sites, (((1,), (1,)), ((), ())), preferred_element_type=F32
    ) * (1.0 / math.sqrt(mapped.shape[-1]))
    top = jnp.max(scores, axis=-1, keepdims=True)
    weights = jnp.exp(scores - top)
    return top, jnp.sum(weights, axis=-1, keepdims=True), dot(weights.astype(BF16), sites)


def joined(left, right):
    top = jnp.maximum(left[0], right[0])
    one, two = jnp.exp(left[0] - top), jnp.exp(right[0] - top)
    return top, left[1] * one + right[1] * two, left[2] * one + right[2] * two


def maps_kernel(q_ref, k_ref, v_ref, o_ref, score_ref, out_ref):
    score_ref[...] = lax.dot_general(
        q_ref[...], k_ref[...], (((1,), (1,)), ((), ())), preferred_element_type=F32
    ).astype(BF16)
    out_ref[...] = dot(v_ref[...], o_ref[...]).astype(BF16)


def query_kernel(own_ref, map_ref, out_ref):
    out_ref[...] = dot(own_ref[...], map_ref[...]).astype(BF16)


def early_kernel(mapped_ref, *refs):
    site_refs, outs = refs[:-3], refs[-3:]
    keep(scored(mapped_ref[...], sites_of(site_refs)), *outs)


def keep(stats, top_ref, total_ref, mixed_ref):
    top, total, mixed_ref[...] = stats
    top_ref[...] = jnp.broadcast_to(top, top_ref.shape)
    total_ref[...] = jnp.broadcast_to(total, total_ref.shape)


def sites_of(refs):
    return refs[0][...] if len(refs) == 1 else jnp.concatenate([ref[...] for ref in refs], axis=0)


def next_kernel(mapped_ref, top_ref, total_ref, mixed_ref, *refs):
    site_refs, outs = refs[:-3], refs[-3:]
    held = top_ref[:, :1], total_ref[:, :1], mixed_ref[...]
    keep(joined(held, scored(mapped_ref[...], sites_of(site_refs))), *outs)


def late_kernel(mapped_ref, top_ref, total_ref, mixed_ref, map_ref, *refs, first, parts):
    site_refs, blocks = refs[:parts], refs[parts:]
    count = blocks[0].shape[0]
    mine = slice(first * count, (first + len(blocks)) * count)
    held = top_ref[mine, :1], total_ref[mine, :1], mixed_ref[mine]
    _, total, mixed = joined(held, scored(mapped_ref[mine], sites_of(site_refs)))
    result = dot((mixed / total).astype(BF16), map_ref[...]).astype(BF16)
    for step, block in enumerate(blocks):
        block[...] = result[step * count : (step + 1) * count]


def sum_kernel(a_ref, b_ref, *refs, group_size):
    *blocks, out_ref = refs
    first, rows, count, channels = a_ref.shape
    place = lax.axis_index(AXIS) // group_size
    for step, block in enumerate(blocks):
        value = block[...].astype(F32).reshape(rows, count, channels)
        frame = place ^ step

        @pl.when(frame < first)
        def _(value=value, frame=frame):
            out_ref[frame] = (a_ref[frame].astype(F32) + value).astype(BF16)

        @pl.when(frame >= first)
        def _(value=value, frame=frame):
            out_ref[frame] = (b_ref[frame - first].astype(F32) + value).astype(BF16)


def call(kernel, outs, scratch, args, flops, spaces=None, sems=(), limit=None):
    vmem = pl.BlockSpec(memory_space=pltpu.VMEM)
    shapes = [jax.ShapeDtypeStruct(shape, dtype) for shape, dtype in outs]
    moved = sum(math.prod(arg.shape) * arg.dtype.itemsize for arg in args)
    moved += sum(math.prod(shape) * jnp.dtype(dtype).itemsize for shape, dtype in outs)
    return pl.pallas_call(
        kernel,
        out_shape=shapes,
        in_specs=[pl.BlockSpec(memory_space=space) for space in spaces or [pltpu.VMEM] * len(args)],
        out_specs=[vmem] * len(outs),
        scratch_shapes=[pltpu.VMEM(shape, dtype) for shape, dtype in scratch] + list(sems),
        compiler_params=pltpu.CompilerParams(vmem_limit_bytes=limit or LIMIT),
        cost_estimate=pl.CostEstimate(flops=int(flops), bytes_accessed=int(moved), transcendentals=0),
    )(*args)


LIMIT = 40 * 1024 * 1024


def per_device(
    video,
    s1_weight,
    t1_weight,
    r1_weight,
    s2_weight,
    t2_weight,
    r2_weight,
    attn_gain,
    w_query,
    w_key,
    w_value,
    w_out,
):
    frames, rows, cols, c0 = video.shape
    c1, c2, c3 = s1_weight.shape[-1], s2_weight.shape[-1], w_out.shape[-1]
    count = cols // PHASES
    devices = lax.axis_size(AXIS)
    group_size = devices // frames
    inner = [(d, d ^ 1) for d in range(devices)]
    groups = lax.axis_size("groups")
    outer = [(d, d + 1) for d in range(1, devices - 1, 2)]
    outer = outer + [(target, source) for source, target in outer]
    outer = [(g * devices + a, g * devices + b) for g in range(groups) for a, b in outer]
    if groups % 2 == 0:
        outer += [
            (g * devices + end, (g ^ 1) * devices + end)
            for g in range(groups)
            for end in (0, devices - 1)
        ]
    turns = [
        [(d, (d // group_size ^ k) * group_size + d % group_size) for d in range(devices)]
        for k in range(frames)
    ]

    edge = ((frames, PHASES, count, c1), BF16)
    taps = ((3, frames, cols, c1), F32)
    dma = pltpu.SemaphoreType.DMA
    site_flops = 2 * frames * cols * 3 * c0 * c1
    held = [pltpu.with_memory_space_constraint(x, pltpu.VMEM) for x in (video, s1_weight)]
    video = pltpu.with_memory_space_constraint(video, pltpu.HBM)
    s1_weight = pltpu.with_memory_space_constraint(s1_weight, pltpu.HBM)
    hbm = pltpu.HBM
    part = frames // 2

    (far_a,) = call(
        first_edge_kernel,
        [((part, *edge[0][1:]), BF16)],
        [((part, cols, c0), BF16), ((3, c0, c1), BF16), taps],
        [video, s1_weight],
        site_flops // 2,
        [hbm] * 2,
        [dma((part,)), dma((3,))],
    )
    far_a = lax.ppermute(far_a, BOTH, outer)
    later = frames - part
    far_b, near = call(
        rest_edge_kernel, [((later, *edge[0][1:]), BF16), edge], [taps], held, site_flops * 1.5
    )
    far_b = lax.ppermute(far_b, BOTH, outer)
    near = lax.ppermute(near, AXIS, inner)
    acc, h_next = call(
        front_kernel, [(edge[0], F32), edge], [edge, taps], [*held, t1_weight], 5 * site_flops
    )
    half = (frames, 2, count, c2)
    d_a, a_one = call(
        functools.partial(far_kernel, first=0),
        [((part, *half[1:]), BF16), ((part, *edge[0][1:]), BF16)],
        [],
        [acc, far_a, h_next, t1_weight, r1_weight],
        1e8,
    )
    far_two = lax.ppermute(d_a, BOTH, outer)
    rest = ((rows // 2 - 1, *half), BF16)
    left_rows = ((rows - 2, *edge[0]), BF16)
    (rest_of,) = call(
        back_rows_kernel,
        [rest],
        [left_rows, left_rows, taps],
        [*held, near, t1_weight, r1_weight],
        9e8,
    )
    near = lax.ppermute(rest_of[-1], AXIS, inner)
    (d_b,) = call(
        functools.partial(far_kernel, first=part),
        [((later, *half[1:]), BF16)],
        [],
        [acc, far_b, h_next, t1_weight, r1_weight, a_one],
        1e8,
    )
    far_two_b = lax.ppermute(d_b, BOTH, outer)
    acc, h_rest = call(
        middle_kernel, [(half, F32), rest], [], [d_a, d_b, rest_of, near, s2_weight, t2_weight], 9e8
    )
    site_rows = rows // 4
    block = ((site_rows * count, c3), BF16)
    gain = attn_gain.reshape(1, c3)
    site = ((part, site_rows, count, c3), BF16)
    residual_a, a_two, normed = call(
        functools.partial(second_kernel, first=0, group_size=group_size),
        [site, ((part, *half[1:]), BF16), site],
        [],
        [acc, far_two, d_a, h_rest, s2_weight, t2_weight, r2_weight, gain],
        3e8,
    )
    residual_b, *blocks = call(
        functools.partial(second_kernel, first=part, group_size=group_size),
        [((later, *site[0][1:]), BF16)] + [block] * frames,
        [],
        [acc, far_two_b, d_b, h_rest, s2_weight, t2_weight, r2_weight, gain, a_two, normed],
        3e8,
    )

    def swap(x, bit):
        return lax.ppermute(x, AXIS, [(d, d ^ bit) for d in range(devices)])

    def join(parts):
        return parts[0] if len(parts) == 1 else jnp.concatenate(parts, axis=0)

    order = (0, frames - 1, *range(1, frames - 1))
    held_blocks = [blocks[0]] + [lax.ppermute(blocks[k], AXIS, turns[k]) for k in order if k]
    own = join(held_blocks)
    bit = group_size // 2
    first_far = [swap(x, bit) for x in held_blocks]
    if bit == 2:
        near_parts, last_parts = first_far[:-1], [first_far[-1]]
        last_parts.append(swap(held_blocks[-1], bit + 1))
    else:
        near_parts, last_parts = [join(first_far)], []
        bit //= 2
        while bit > 1:
            near_parts.append(swap(join([own] + near_parts), bit))
            bit //= 2
    weight = ((c3, c3), BF16)
    score_map, out_map = call(
        maps_kernel, [weight, weight], [], [w_query, w_key, w_value, w_out], 5e8
    )
    partner = swap(own, 1)
    (mapped,) = call(query_kernel, [(own.shape, BF16)], [], [own, score_map], 1e8)
    stats = ((own.shape[0], 128), F32)
    sums = [stats, stats, (own.shape, F32)]
    early = call(early_kernel, sums, [], [mapped, own, partner], 3e8)
    near_parts, early = lax.optimization_barrier((near_parts, early))
    far_sites = join(near_parts)
    last_parts.append(swap(far_sites, 1))
    held_sums = call(next_kernel, sums, [], [mapped, *early, far_sites], 2e8)

    def late_blocks(first, after):
        return call(
            functools.partial(late_kernel, first=first, parts=len(last_parts)),
            [block] * (after - first),
            [],
            [mapped, *held_sums, out_map, *last_parts],
            3e8,
        )

    done = dict(zip(order, late_blocks(0, frames)))
    blocks = [done[0]] + [lax.ppermute(done[k], AXIS, turns[k]) for k in range(1, frames)]
    (encoded,) = call(
        functools.partial(sum_kernel, group_size=group_size),
        [((frames, site_rows, count, c3), BF16)],
        [],
        [residual_a, residual_b, *blocks],
        1e6,
    )
    return encoded


def solution(mesh):
    placed = (P("groups", "ha", None, None), P(), P(), P(), P(), P(), P(), P(), P(), P(), P(), P())
    return jax.shard_map(
        per_device,
        mesh=mesh,
        in_specs=placed,
        out_specs=P("groups", "ha", None, None),
        check_vma=False,
    )
```

```python
import functools
import math

import jax
import jax.numpy as jnp
from jax import lax
from jax.experimental import pallas as pl
from jax.experimental.pallas import tpu as pltpu
from jax.sharding import PartitionSpec as P


F32 = jnp.float32
BF16 = jnp.bfloat16
AXIS = "ha"
BOTH = ("groups", AXIS)
PHASES = 4


def dot(left, right):
    return jnp.dot(left, right, preferred_element_type=F32)


def turn():
    return lax.axis_index(AXIS) % 2


def whole_row(row, count):
    return row + turn() * (count - 1 - 2 * row)


def inside(far):
    index = lax.axis_index(AXIS)
    at_end = (index == 0) | (index == lax.axis_size(AXIS) - 1)
    return jnp.where(at_end, jnp.zeros_like(far), far)


def causal(a, t_ref, first=0):
    frames, sites, channels = a.shape
    total = None
    for lag in range(3):
        start = max(first - lag, 0)
        held = a[start : frames - lag]
        count = held.shape[0]
        if not count:
            continue
        term = dot(held.reshape(count * sites, channels), t_ref[2 - lag]).reshape(count, sites, -1)
        skip = frames - first - count
        if total is None:
            total = term
        elif skip:
            total = jnp.concatenate([total[:skip], total[skip:] + term], axis=0)
        else:
            total = total + term
    return total


def causal_pairs(a, t_ref, first=0):
    frames, _, channels = a.shape
    none = jnp.zeros_like(t_ref[0])
    results = []
    for frame in range(first, frames, 2):
        held = range(max(frame - 2, 0), frame + 2)

        def tap(source, target):
            lag = target - source
            return t_ref[2 - lag] if 0 <= lag <= 2 else none

        weight = jnp.concatenate(
            [lanes([tap(source, frame), tap(source, frame + 1)]) for source in held], axis=0
        )
        both = dot(lanes([a[source] for source in held]), weight)
        results += [both[:, :channels], both[:, channels:]]
    return jnp.stack(results, axis=0)


def reduction(r_ref):
    first = turn()
    return jnp.concatenate(
        [r_ref[first, 0], r_ref[first, 1], r_ref[1 - first, 0], r_ref[1 - first, 1]], axis=0
    )


def lanes(parts):
    return parts[0] if len(parts) == 1 else jnp.concatenate(parts, axis=-1)


def silu(x):
    return 0.5 * x * (1.0 + jnp.tanh(0.5 * x))


def shifted(x, step, period):
    rows, channels = x.shape
    place = lax.broadcasted_iota(jnp.int32, (rows // period, period, channels), 1)
    place = place.reshape(rows, channels)
    moved = pltpu.roll(x, step % rows, 0)
    return jnp.where(place == (0 if step == 1 else period - 1), 0.0, moved)


def place_phases(total, tap_ref, out_of):
    _, frames, cols, channels = tap_ref.shape
    count = cols // PHASES
    for tap in range(3):
        tap_ref[tap] = total[:, tap * channels : (tap + 1) * channels].reshape(
            frames, cols, channels
        )
    for frame in range(frames):
        def strided(tap, phase):
            return tap_ref[tap, frame, pl.ds(phase, count, stride=PHASES), :]

        for phase in range(PHASES):
            before = (
                shifted(strided(0, PHASES - 1), 1, count)
                if phase == 0
                else strided(0, phase - 1)
            )
            after = (
                shifted(strided(2, 0), -1, count)
                if phase == PHASES - 1
                else strided(2, phase + 1)
            )
            out_of(frame, phase, before + strided(1, phase) + after)


def tap_matrix(w_ref, row):
    return lanes([w_ref[row, tap] for tap in range(3)])


def fetch_rows(video_ref, row, first, rows_to, sem):
    copies = [
        pltpu.make_async_copy(video_ref.at[first + at, row], rows_to.at[at], sem.at[at])
        for at in range(rows_to.shape[0])
    ]
    for copy in copies:
        copy.start()
    return copies


def fetch_taps(w_ref, tap, taps_to, sem):
    copies = [
        pltpu.make_async_copy(w_ref.at[tap, column], taps_to.at[column], sem.at[column])
        for column in range(taps_to.shape[0])
    ]
    for copy in copies:
        copy.start()
    return copies


def finish(copies):
    for copy in copies:
        copy.wait()


def edge_of(rows, taps_ref, tap_ref, out_ref):
    frames, cols, channels = rows.shape
    weight = lanes([taps_ref[column] for column in range(3)])
    total = dot(rows.reshape(frames * cols, channels), weight)

    def store(frame, phase, value):
        out_ref[frame, phase] = value.astype(BF16)

    place_phases(total, tap_ref.at[:, :frames], store)


def first_edge_kernel(video_ref, w_ref, out_ref, rows_to, taps_to, tap_ref, row_sem, tap_sem):
    side = turn()
    row = whole_row(0, video_ref.shape[1])
    copies = fetch_taps(w_ref, 2 - 2 * side, taps_to, tap_sem)
    finish(fetch_rows(video_ref, row, 0, rows_to, row_sem) + copies)
    edge_of(rows_to[...], taps_to, tap_ref, out_ref)


def rest_edge_kernel(video_ref, w_ref, far_out, near_out, tap_ref):
    frames, rows = video_ref.shape[:2]
    side = turn()
    first = frames - far_out.shape[0]
    far = video_ref[first:, whole_row(0, rows)]
    edge_of(far, w_ref.at[2 - 2 * side], tap_ref, far_out)
    edge_of(video_ref[:, whole_row(rows - 1, rows)], w_ref.at[2 * side], tap_ref, near_out)


def inner_rows(wanted, video_ref, w_ref, tap_ref, store_of):
    frames, rows, cols, channels = video_ref.shape
    side = turn()
    taps = {0: 1, -1: 2 * side, 1: 2 - 2 * side}
    totals = {}
    for source in range(max(wanted[0] - 1, 0), min(wanted[-1] + 2, rows)):
        steps = [step for step in taps if source - step in wanted]
        weight = lanes([tap_matrix(w_ref, taps[step]) for step in steps])
        held = video_ref[:, whole_row(source, rows)].reshape(frames * cols, channels)
        terms = dot(held, weight)
        wide = terms.shape[-1] // len(steps)
        for at, step in enumerate(steps):
            term = terms[:, at * wide : (at + 1) * wide]
            row = source - step
            totals[row] = totals[row] + term if row in totals else term
    for row in wanted:
        place_phases(totals[row], tap_ref, store_of(row))


def front_kernel(video_ref, w_ref, t_ref, acc_ref, h_ref, one_ref, tap_ref):
    frames, phases, count, channels = acc_ref.shape

    def store_of(row):
        def store(frame, phase, value):
            if row == 0:
                acc_ref[frame, phase] = value
            else:
                one_ref[frame, phase] = value.astype(BF16)

        return store

    inner_rows((0, 1), video_ref, w_ref, tap_ref, store_of)
    a = one_ref[...].reshape(frames, phases * count, channels)
    h_ref[...] = silu(causal_pairs(a, t_ref)).astype(BF16).reshape(h_ref.shape)


def to_half(h, weight, frames, phases, count):
    return [
        dot(lanes([h(row, 2 * side + j) for row in range(2) for j in range(2)]), weight)
        .astype(BF16)
        .reshape(frames, count, -1)
        for side in range(phases // 2)
    ]


def far_kernel(acc_ref, far_ref, h_in, t_ref, r_ref, *refs, first):
    frames, phases, count, channels = far_ref.shape
    mine = pl.ds(first, frames)
    a = (acc_ref[mine] + inside(far_ref[...].astype(F32))).astype(BF16)
    if first:
        before_ref, d_ref = refs
        whole = jnp.concatenate([before_ref[...], a], axis=0)
    else:
        d_ref, a_ref = refs
        a_ref[...] = a
        whole = a
    whole = whole.reshape(whole.shape[0], phases * count, channels)
    h = silu(causal(whole, t_ref, first)).astype(BF16).reshape(frames, phases, count, channels)
    parts = to_half(
        lambda row, phase: (h_in[mine, phase] if row else h[:, phase]).reshape(
            frames * count, channels
        ),
        reduction(r_ref),
        frames,
        phases,
        count,
    )
    for side, part in enumerate(parts):
        d_ref[:, side] = part


def back_rows_kernel(
    video_ref, w_ref, near_ref, t_ref, r_ref, d_ref, acc_ref, h_ref, tap_ref
):
    frames, phases, count, channels = near_ref.shape
    last = video_ref.shape[1] - 1

    def store_of(row):
        def store(frame, phase, value):
            if row == last:
                value = value + near_ref[frame, phase].astype(F32)
            acc_ref[row - 2, frame, phase] = value.astype(BF16)

        return store

    inner_rows(range(2, last + 1), video_ref, w_ref, tap_ref, store_of)
    for row in range(2, last + 1):
        a = acc_ref[row - 2].reshape(frames, phases * count, channels)
        h_ref[row - 2] = silu(causal(a, t_ref)).astype(BF16).reshape(h_ref.shape[1:])
    weight = reduction(r_ref)
    for half in range(d_ref.shape[0]):
        parts = to_half(
            lambda row, phase: h_ref[2 * half + row, :, phase].reshape(frames * count, channels),
            weight,
            frames,
            phases,
            count,
        )
        for side, part in enumerate(parts):
            d_ref[half, :, side] = part


def place_pairs(total, sites, count, channels):
    even, odd = total[:sites], total[sites:]
    first, middle, last = (slice(tap * channels, (tap + 1) * channels) for tap in range(3))
    return (
        shifted(odd[:, first], 1, count) + even[:, middle] + odd[:, last],
        even[:, first] + odd[:, middle] + shifted(even[:, last], -1, count),
    )


def flat(d):
    frames, sides, count, channels = d.shape
    return jnp.concatenate(
        [d[:, side].reshape(frames * count, channels) for side in range(sides)], axis=0
    )


def by_side(pair, shape):
    frames, _, count, channels = shape
    return jnp.stack([value.reshape(frames, count, channels) for value in pair], axis=1)


def second_rows(a, d, t_ref, first=0):
    _, sides, count, channels = d.shape
    mixed = silu(causal(a.reshape(a.shape[0], sides * count, channels), t_ref, first))
    return (d.astype(F32) + mixed.reshape(d.shape)).astype(BF16)


def middle_kernel(far_a_ref, far_b_ref, rest_ref, near_ref, w_ref, t_ref, acc_ref, h_ref):
    shape = near_ref.shape
    frames, _, count, channels = shape
    sites = frames * count
    rows = rest_ref.shape[0] + 1
    side = turn()
    taps = {-1: 2 * side, 0: 1, 1: 2 - 2 * side}
    held = [jnp.concatenate([far_a_ref[...], far_b_ref[...]], axis=0)]
    held += [rest_ref[row] for row in range(rows - 1)] + [near_ref[...]]
    for row in range(rows):
        total = None
        for step, tap in taps.items():
            if row + step >= 0:
                term = dot(flat(held[row + step]), tap_matrix(w_ref, tap))
                total = term if total is None else total + term
        a = by_side(place_pairs(total, sites, count, channels), shape)
        if row == 0:
            acc_ref[...] = a
        else:
            h_ref[row - 1] = second_rows(a.astype(BF16), held[row], t_ref)


def second_kernel(
    acc_ref, far_ref, d_ref, rest_ref, w_ref, t_ref, r_ref, gain_ref, *refs, first, group_size
):
    shape = d_ref.shape
    frames, _, count, channels = shape
    sites = frames * count
    mine = pl.ds(first, frames)
    more = dot(flat(inside(far_ref[...])), tap_matrix(w_ref, 2 * turn()))
    a = acc_ref[mine] + by_side(place_pairs(more, sites, count, channels), shape)
    a = a.astype(BF16)
    if first:
        before_ref, done_ref, h_out, *blocks = refs
        whole = jnp.concatenate([before_ref[...], a], axis=0)
    else:
        h_out, a_out, normed_out = refs
        a_out[...] = a
        whole = a
    held = [second_rows(whole, d_ref[...], t_ref, first)]
    held += [rest_ref[row, mine] for row in range(rest_ref.shape[0])]
    weight = reduction(r_ref)
    wide = weight.shape[-1]
    gain = gain_ref[...].astype(F32)
    place = lax.axis_index(AXIS) // group_size
    halves = len(held) // 2
    for half in range(halves):
        left = lanes(
            [held[2 * half + i][:, j].reshape(sites, channels) for i in range(2) for j in range(2)]
        )
        out_row = whole_row(half, halves) if halves > 1 else 0
        residual = dot(left, weight).astype(BF16)
        h_out[:, out_row] = residual.reshape(frames, count, wide)
        residual = residual.astype(F32)
        mean_square = jnp.mean(residual * residual, axis=-1, keepdims=True)
        normed = (residual * lax.rsqrt(mean_square + 1e-06) * gain).astype(BF16)
        normed = normed.reshape(frames, count, wide)
        if not first:
            normed_out[:, out_row] = normed
            continue
        ready = [done_ref[frame, out_row] for frame in range(first)]
        ready += [normed[frame] for frame in range(frames)]
        for frame, value in enumerate(ready):
            for step, block in enumerate(blocks):

                @pl.when(place ^ step == frame)
                def _(block=block, value=value, out_row=out_row):
                    at = out_row * count if halves > 1 else 0
                    block[pl.ds(at, count), :] = value


def scored(mapped, sites):
    scores = lax.dot_general(
        mapped, sites, (((1,), (1,)), ((), ())), preferred_element_type=F32
    ) * (1.0 / math.sqrt(mapped.shape[-1]))
    top = jnp.max(scores, axis=-1, keepdims=True)
    weights = jnp.exp(scores - top)
    return top, jnp.sum(weights, axis=-1, keepdims=True), dot(weights.astype(BF16), sites)


def joined(left, right):
    top = jnp.maximum(left[0], right[0])
    one, two = jnp.exp(left[0] - top), jnp.exp(right[0] - top)
    return top, left[1] * one + right[1] * two, left[2] * one + right[2] * two


def maps_kernel(q_ref, k_ref, v_ref, o_ref, score_ref, out_ref):
    score_ref[...] = lax.dot_general(
        q_ref[...], k_ref[...], (((1,), (1,)), ((), ())), preferred_element_type=F32
    ).astype(BF16)
    out_ref[...] = dot(v_ref[...], o_ref[...]).astype(BF16)


def query_kernel(own_ref, map_ref, out_ref):
    out_ref[...] = dot(own_ref[...], map_ref[...]).astype(BF16)


def early_kernel(mapped_ref, *refs):
    site_refs, outs = refs[:-3], refs[-3:]
    keep(scored(mapped_ref[...], sites_of(site_refs)), *outs)


def keep(stats, top_ref, total_ref, mixed_ref):
    top, total, mixed_ref[...] = stats
    top_ref[...] = jnp.broadcast_to(top, top_ref.shape)
    total_ref[...] = jnp.broadcast_to(total, total_ref.shape)


def sites_of(refs):
    return refs[0][...] if len(refs) == 1 else jnp.concatenate([ref[...] for ref in refs], axis=0)


def late_kernel(mapped_ref, top_ref, total_ref, mixed_ref, map_ref, *refs, first, parts):
    site_refs, blocks = refs[:parts], refs[parts:]
    count = blocks[0].shape[0]
    mine = slice(first * count, (first + len(blocks)) * count)
    held = top_ref[mine, :1], total_ref[mine, :1], mixed_ref[mine]
    _, total, mixed = joined(held, scored(mapped_ref[mine], sites_of(site_refs)))
    result = dot((mixed / total).astype(BF16), map_ref[...]).astype(BF16)
    for step, block in enumerate(blocks):
        block[...] = result[step * count : (step + 1) * count]


def sum_kernel(a_ref, b_ref, *refs, group_size):
    *blocks, out_ref = refs
    first, rows, count, channels = a_ref.shape
    place = lax.axis_index(AXIS) // group_size
    for step, block in enumerate(blocks):
        value = block[...].astype(F32).reshape(rows, count, channels)
        frame = place ^ step

        @pl.when(frame < first)
        def _(value=value, frame=frame):
            out_ref[frame] = (a_ref[frame].astype(F32) + value).astype(BF16)

        @pl.when(frame >= first)
        def _(value=value, frame=frame):
            out_ref[frame] = (b_ref[frame - first].astype(F32) + value).astype(BF16)


def call(kernel, outs, scratch, args, flops, spaces=None, sems=(), limit=None):
    vmem = pl.BlockSpec(memory_space=pltpu.VMEM)
    shapes = [jax.ShapeDtypeStruct(shape, dtype) for shape, dtype in outs]
    moved = sum(math.prod(arg.shape) * arg.dtype.itemsize for arg in args)
    moved += sum(math.prod(shape) * jnp.dtype(dtype).itemsize for shape, dtype in outs)
    return pl.pallas_call(
        kernel,
        out_shape=shapes,
        in_specs=[pl.BlockSpec(memory_space=space) for space in spaces or [pltpu.VMEM] * len(args)],
        out_specs=[vmem] * len(outs),
        scratch_shapes=[pltpu.VMEM(shape, dtype) for shape, dtype in scratch] + list(sems),
        compiler_params=pltpu.CompilerParams(vmem_limit_bytes=limit or LIMIT),
        cost_estimate=pl.CostEstimate(flops=int(flops), bytes_accessed=int(moved), transcendentals=0),
    )(*args)


LIMIT = 40 * 1024 * 1024


def per_device(
    video,
    s1_weight,
    t1_weight,
    r1_weight,
    s2_weight,
    t2_weight,
    r2_weight,
    attn_gain,
    w_query,
    w_key,
    w_value,
    w_out,
):
    frames, rows, cols, c0 = video.shape
    c1, c2, c3 = s1_weight.shape[-1], s2_weight.shape[-1], w_out.shape[-1]
    count = cols // PHASES
    devices = lax.axis_size(AXIS)
    group_size = devices // frames
    inner = [(d, d ^ 1) for d in range(devices)]
    groups = lax.axis_size("groups")
    outer = [(d, d + 1) for d in range(1, devices - 1, 2)]
    outer = outer + [(target, source) for source, target in outer]
    outer = [(g * devices + a, g * devices + b) for g in range(groups) for a, b in outer]
    if groups % 2 == 0:
        outer += [
            (g * devices + end, (g ^ 1) * devices + end)
            for g in range(groups)
            for end in (0, devices - 1)
        ]
    turns = [
        [(d, (d // group_size ^ k) * group_size + d % group_size) for d in range(devices)]
        for k in range(frames)
    ]

    edge = ((frames, PHASES, count, c1), BF16)
    taps = ((3, frames, cols, c1), F32)
    dma = pltpu.SemaphoreType.DMA
    site_flops = 2 * frames * cols * 3 * c0 * c1
    held = [pltpu.with_memory_space_constraint(x, pltpu.VMEM) for x in (video, s1_weight)]
    video = pltpu.with_memory_space_constraint(video, pltpu.HBM)
    s1_weight = pltpu.with_memory_space_constraint(s1_weight, pltpu.HBM)
    hbm = pltpu.HBM
    part = frames // 2

    (far_a,) = call(
        first_edge_kernel,
        [((part, *edge[0][1:]), BF16)],
        [((part, cols, c0), BF16), ((3, c0, c1), BF16), taps],
        [video, s1_weight],
        site_flops // 2,
        [hbm] * 2,
        [dma((part,)), dma((3,))],
    )
    far_a = lax.ppermute(far_a, BOTH, outer)
    later = frames - part
    far_b, near = call(
        rest_edge_kernel, [((later, *edge[0][1:]), BF16), edge], [taps], held, site_flops * 1.5
    )
    far_b = lax.ppermute(far_b, BOTH, outer)
    near = lax.ppermute(near, AXIS, inner)
    acc, h_next = call(
        front_kernel, [(edge[0], F32), edge], [edge, taps], [*held, t1_weight], 5 * site_flops
    )
    half = (frames, 2, count, c2)
    d_a, a_one = call(
        functools.partial(far_kernel, first=0),
        [((part, *half[1:]), BF16), ((part, *edge[0][1:]), BF16)],
        [],
        [acc, far_a, h_next, t1_weight, r1_weight],
        1e8,
    )
    far_two = lax.ppermute(d_a, BOTH, outer)
    rest = ((rows // 2 - 1, *half), BF16)
    left_rows = ((rows - 2, *edge[0]), BF16)
    (rest_of,) = call(
        back_rows_kernel,
        [rest],
        [left_rows, left_rows, taps],
        [*held, near, t1_weight, r1_weight],
        9e8,
    )
    near = lax.ppermute(rest_of[-1], AXIS, inner)
    (d_b,) = call(
        functools.partial(far_kernel, first=part),
        [((later, *half[1:]), BF16)],
        [],
        [acc, far_b, h_next, t1_weight, r1_weight, a_one],
        1e8,
    )
    far_two_b = lax.ppermute(d_b, BOTH, outer)
    acc, h_rest = call(
        middle_kernel, [(half, F32), rest], [], [d_a, d_b, rest_of, near, s2_weight, t2_weight], 9e8
    )
    site_rows = rows // 4
    block = ((site_rows * count, c3), BF16)
    gain = attn_gain.reshape(1, c3)
    site = ((part, site_rows, count, c3), BF16)
    residual_a, a_two, normed = call(
        functools.partial(second_kernel, first=0, group_size=group_size),
        [site, ((part, *half[1:]), BF16), site],
        [],
        [acc, far_two, d_a, h_rest, s2_weight, t2_weight, r2_weight, gain],
        3e8,
    )
    residual_b, *blocks = call(
        functools.partial(second_kernel, first=part, group_size=group_size),
        [((later, *site[0][1:]), BF16)] + [block] * frames,
        [],
        [acc, far_two_b, d_b, h_rest, s2_weight, t2_weight, r2_weight, gain, a_two, normed],
        3e8,
    )

    def swap(x, bit):
        return lax.ppermute(x, AXIS, [(d, d ^ bit) for d in range(devices)])

    def join(parts):
        return parts[0] if len(parts) == 1 else jnp.concatenate(parts, axis=0)

    order = (0, frames - 1, *range(1, frames - 1))
    held_blocks = [blocks[0]] + [lax.ppermute(blocks[k], AXIS, turns[k]) for k in order if k]
    own = join(held_blocks)
    bit = group_size // 2
    first_far = [swap(x, bit) for x in held_blocks]
    if bit == 2:
        near_parts, last_parts = first_far[:-1], [first_far[-1]]
        last_parts.append(swap(held_blocks[-1], bit + 1))
    else:
        near_parts, last_parts = [join(first_far)], []
        bit //= 2
        while bit > 1:
            near_parts.append(swap(join([own] + near_parts), bit))
            bit //= 2
    weight = ((c3, c3), BF16)
    score_map, out_map = call(
        maps_kernel, [weight, weight], [], [w_query, w_key, w_value, w_out], 5e8
    )
    partner = swap(own, 1)
    (mapped,) = call(query_kernel, [(own.shape, BF16)], [], [own, score_map], 1e8)
    stats = ((own.shape[0], 128), F32)
    sums = [stats, stats, (own.shape, F32)]
    early = call(early_kernel, sums, [], [mapped, own, partner], 3e8)
    near_parts, early = lax.optimization_barrier((near_parts, early))
    far_sites = join(near_parts)
    last_parts.append(swap(far_sites, 1))
    last_parts.append(far_sites)

    def late_blocks(first, after):
        return call(
            functools.partial(late_kernel, first=first, parts=len(last_parts)),
            [block] * (after - first),
            [],
            [mapped, *early, out_map, *last_parts],
            3e8,
        )

    done = dict(zip(order, late_blocks(0, frames)))
    blocks = [done[0]] + [lax.ppermute(done[k], AXIS, turns[k]) for k in range(1, frames)]
    (encoded,) = call(
        functools.partial(sum_kernel, group_size=group_size),
        [((frames, site_rows, count, c3), BF16)],
        [],
        [residual_a, residual_b, *blocks],
        1e6,
    )
    return encoded


def solution(mesh):
    placed = (P("groups", "ha", None, None), P(), P(), P(), P(), P(), P(), P(), P(), P(), P(), P())
    return jax.shard_map(
        per_device,
        mesh=mesh,
        in_specs=placed,
        out_specs=P("groups", "ha", None, None),
        check_vma=False,
    )
```
